32 devices in a mesh: dp: 8 (over y, x, core), tensor: 4 (over z).
Axes of the slice: x: 2, y: 2, z: 4, core: 2. Of those that a mesh axis runs over, the one named last changes fastest.
Arguments:
- picture_encoder_result: bfloat16 [2816, 1024], P('dp'), may hold values from -0.59765625 to 0.59765625
- sentence_encoder_result: bfloat16 [11264, 1024], P(('dp', 'tensor')), may hold values from -0.59765625 to 0.59765625
- picture_projector_matrix: bfloat16 [1024, 1024], P(None, 'tensor'), may hold values from -0.1875 to 0.1875
- sentence_projector_matrix: bfloat16 [1024, 1024], P(None, 'tensor'), may hold values from -0.1875 to 0.1875
- sentences_for_picture: int32 [2816], replicated, may hold values from 1 to 8, 11264 in all
- sharpness_factor: float32 [1], replicated, may hold values from 30 to 60
- score_offset_term: float32 [1], replicated, may hold values from -8 to -4
Outputs:
- grad_img: bfloat16 [2816, 1024], P('dp', 'tensor')
- grad_cap: bfloat16 [11264, 1024], P(('dp', 'tensor'))
The draws below stay inside these ranges and needn't reach their ends.
Inputs may be any that keep to these rules, and one draw needn't show every extreme that they name: The counts sum to 11264; the captions of image m are the consecutive rows start[m] to start[m] + sentences_for_picture[m] - 1 of sentence_encoder_result, where start[m] is the sum of the counts of images before m; some image has 8.
All inputs are finite; a program needn't handle non-finite values.
Results may differ from the reference program's by a relative error of at most 0.014.
Values may be sent and summed in bfloat16 or wider, within the bound.
No kernel may reach another device: no remote copies, remote signals or barrier semaphores. Data moves between devices by JAX's collectives and lax.ppermute only.
A program may use at most 64 MiB of HBM per device.

```python
import math
import jax
import jax.numpy as jnp
import numpy as np
from jax import lax

D = 1024
E = 1024
IMG_DEV = 352
IMAGES = 2816
CAPS = 11264
N_DP = 8


def block_levels(own_key, shape, split, smallest, largest):
    factor_of = 1.0
    for dim, shards_of in split:
        heights = jax.random.uniform(jax.random.fold_in(jax.random.fold_in(own_key, 6), dim), (shards_of,), jnp.float32, smallest / len(split), largest / len(split))
        factor_of = factor_of * jnp.repeat(jnp.exp(heights), shape[dim] // shards_of).reshape((-1,) + (1,) * (len(shape) - 1 - dim))
    return factor_of


def length_profile(amount, total, reach, lean):
    weights = [(1 << 20) // math.isqrt(grade ** lean) + 1 for grade in range(2, amount + 1)]
    surplus, given = total - reach - (amount - 1), [1] * (amount - 1)
    while surplus > 0:
        movable = [i for i in range(amount - 1) if given[i] < reach]
        whole, budget = sum([weights[i] for i in movable]), surplus
        for i in movable:
            addition = min(reach - given[i], max(1, budget * weights[i] // whole), surplus)
            given[i] = given[i] + addition
            surplus = surplus - addition
    return np.array([reach] + given)


def uneven_parts(stream_key, count, total, reach, skew):
    if count == 2:
        one = jax.random.randint(stream_key, (), max(1, total - reach), min(reach, total - 1) + 1)
        return jnp.stack([one, total - one])
    sizes = jnp.asarray(length_profile(count, total, reach, skew), jnp.int32)
    couples = (count - 1) // 2
    donor, sink = sizes[1:1 + 2 * couples:2], sizes[2:2 + 2 * couples:2]
    slack = jnp.minimum(donor - 1, reach - sink)
    moved = jax.random.randint(jax.random.fold_in(stream_key, 1), (couples,), 0, 1 << 20) % (slack + 1)
    sizes = sizes.at[1:1 + 2 * couples:2].set(donor - moved).at[2:2 + 2 * couples:2].set(sink + moved)
    return sizes[jax.random.permutation(jax.random.fold_in(stream_key, 2), count)]


def bell_draw(stream_key, extent, width, bound, pieces=(), kind=jnp.bfloat16):
    gain = block_levels(stream_key, extent, pieces, -0.22, 0.18) if pieces else 1.0
    entries = jax.random.normal(stream_key, extent, jnp.float32) * width * gain
    return jnp.minimum(jnp.maximum(entries, -bound), bound).astype(kind)


def setup_inputs(seed: int = 0) -> dict:
    seeds = jax.random.split(jax.random.key(seed), 8)
    picture_encoder_result = bell_draw(seeds[0], (IMAGES, D), 0.1, 0.59765625, ((0, 8),))
    sentence_encoder_result = bell_draw(seeds[1], (CAPS, D), 0.1, 0.59765625, ((0, 32),))
    picture_projector_matrix = bell_draw(seeds[2], (D, E), D ** -0.5, 0.1875, ((1, 4),))
    sentence_projector_matrix = bell_draw(seeds[3], (D, E), D ** -0.5, 0.1875, ((1, 4),))
    sentences_for_picture = uneven_parts(seeds[4], IMAGES, CAPS, 8, 1).astype(jnp.int32)
    sharpness_factor = jnp.clip(jax.random.uniform(seeds[5], (1,), jnp.float32, 30.0, 60.0), 30.0, 60.0)
    score_offset_term = jnp.clip(jax.random.uniform(seeds[6], (1,), jnp.float32, -8.0, -4.0), -8.0, -4.0)
    return {"picture_encoder_result": picture_encoder_result, "sentence_encoder_result": sentence_encoder_result, "picture_projector_matrix": picture_projector_matrix, "sentence_projector_matrix": sentence_projector_matrix, "sentences_for_picture": sentences_for_picture, "sharpness_factor": sharpness_factor, "score_offset_term": score_offset_term}


epsilon = 1e-06

def embed(features, loss_multiplier):
    raw = jnp.dot(features, loss_multiplier, preferred_element_type=jnp.float32)
    scale = lax.rsqrt(lax.optimization_barrier(jnp.sum(raw * raw, axis=1, keepdims=True)) + epsilon)
    return (raw * scale, scale)

def scaling_factor(similarity_matrix, other_begin_list, sentence_tally_later, other_position, scaled_sharpness, displacement):
    raw_similarity = scaled_sharpness * similarity_matrix + displacement
    inside = (other_position >= other_begin_list) & (other_position < other_begin_list + sentence_tally_later)
    match_polarity = jnp.where(inside, 1.0, -1.0)
    loss_multiplier = jnp.where(inside, 1.0 / sentence_tally_later.astype(jnp.float32), 1.0)
    return (scaled_sharpness * (-match_polarity * loss_multiplier * jax.nn.sigmoid(-match_polarity * raw_similarity))).astype(jnp.bfloat16)

def unit_back(grad, unit, scale):
    return scale * (grad - unit * lax.optimization_barrier(jnp.sum(unit * grad, axis=1, keepdims=True)))

def reference(picture_encoder_result, sentence_encoder_result, picture_projector_matrix, sentence_projector_matrix, sentences_for_picture, sharpness_factor, score_offset_term):
    img_unit, img_scale = embed(picture_encoder_result, picture_projector_matrix)
    cap_unit, cap_scale = embed(sentence_encoder_result, sentence_projector_matrix)
    img_z = img_unit.astype(jnp.bfloat16)
    cap_z = cap_unit.astype(jnp.bfloat16)
    ends = jnp.cumsum(sentences_for_picture).astype(jnp.int32)
    starts = (ends - sentences_for_picture).astype(jnp.int32)
    sentence_number = jnp.arange(CAPS, dtype=jnp.int32)
    scaled_sharpness = sharpness_factor[0]
    displacement = score_offset_term[0]

    def scan_step(cap_grad, block):
        block_z, group_begin_list, group_sizes_list = block
        similarity_matrix = jnp.dot(block_z, cap_z.T, preferred_element_type=jnp.float32)
        pair_factor = scaling_factor(similarity_matrix, group_begin_list[:, None], group_sizes_list[:, None], sentence_number[None, :], scaled_sharpness, displacement)
        block_grad = jnp.dot(pair_factor, cap_z, preferred_element_type=jnp.float32)
        cap_grad = cap_grad + jnp.dot(pair_factor.T, block_z, preferred_element_type=jnp.float32)
        return (cap_grad, block_grad)
    cap_grad, img_grad = lax.scan(scan_step, jnp.zeros((CAPS, E), jnp.float32), (img_z.reshape(N_DP, IMG_DEV, E), starts.reshape(N_DP, IMG_DEV), sentences_for_picture.reshape(N_DP, IMG_DEV)))
    img_grad = img_grad.reshape(IMAGES, E)
    img_back = unit_back(img_grad, img_unit, img_scale)
    cap_back = unit_back(cap_grad, cap_unit, cap_scale)
    grad_img = jnp.dot(img_back, picture_projector_matrix.astype(jnp.float32).T, precision=lax.Precision.HIGHEST)
    grad_cap = jnp.dot(cap_back, sentence_projector_matrix.astype(jnp.float32).T, precision=lax.Precision.HIGHEST)
    return (grad_img.astype(jnp.bfloat16), grad_cap.astype(jnp.bfloat16))
```

```python
import functools

import jax
import jax.numpy as jnp
from jax import lax
from jax.experimental import pallas as pl
from jax.experimental.pallas import tpu as pltpu
from jax.sharding import PartitionSpec as P

epsilon = 1e-06
CORES = 2
ROWS_Y = 2
F32 = jnp.float32
BF16 = jnp.bfloat16


def contract_last(a, b):
    return lax.dot_general(a, b, (((1,), (1,)), ((), ())), preferred_element_type=F32)


def contract_first(a, b):
    return lax.dot_general(a, b, (((0,), (0,)), ((), ())), preferred_element_type=F32)


def front_kernel(lay, *refs):
    n_cap, n_img, n_pc, n_pi = lay["n_cap"], lay["n_img"], lay["n_pc"], lay["n_pi"]
    rows, img_rows = lay["rows"], lay["img_rows"]
    slots, width = lay["slots"], lay["width"]
    at = 0

    def take(count):
        nonlocal at
        got = refs[at : at + count]
        at += count
        return got

    (place,) = take(1)
    cap_x = take(n_cap)
    img_x = take(n_img)
    (wc_own,) = take(1)
    wc_pieces = take((slots - 1) * n_pc)
    (wi_own,) = take(1)
    wi_pieces = take((slots - 1) * n_pi)
    first, last, weight, position, factors = take(5)
    out_img_send, out_img_own, out_cap_core, out_cap_next, out_cap_own, wc, wi = take(7)
    xc, xi, zc, zi, raw_c, raw_i, sc_c, sc_i, logits, coef, dz, dzc, sem = take(13)

    depth = wc.shape[0]
    copies_c, copies_i = [], []

    def start(src, dst, group, index):
        copy = pltpu.make_async_copy(src, dst, sem.at[index])
        copy.start()
        group.append(copy)

    index = 0
    for own, pieces, full, n_p, base, group in (
        (wc_own, wc_pieces, wc, n_pc, 0, copies_c),
        (wi_own, wi_pieces, wi, n_pi, n_pc, copies_i),
    ):
        step = depth // n_p
        start(own, full.at[:, pl.ds(0, width)], group, index)
        index += 1
        for k in range(1, slots):
            for r in range(n_p):
                offset = pl.multiple_of(place[base + r], step)
                start(
                    pieces[(k - 1) * n_p + r],
                    full.at[pl.ds(offset, step), pl.ds(k * width, width)],
                    group,
                    index,
                )
                index += 1
    for q in range(n_cap):
        start(cap_x[q], xc.at[pl.ds(q * rows, rows), :], copies_c, index)
        index += 1
    for q in range(n_img):
        start(img_x[q], xi.at[pl.ds(q * img_rows, img_rows), :], copies_i, index)
        index += 1

    def forward(x, w, raw, z, scales, blocks, rows):
        def block(q, _):
            at_row = pl.multiple_of(q * rows, 16)
            raw[pl.ds(at_row, rows), :] = jnp.dot(
                x[pl.ds(at_row, rows), :], w[...], preferred_element_type=F32
            )

            def chunk(r, _):
                here = pl.multiple_of(at_row + r * 16, 16)
                value = raw[pl.ds(here, 16), :]
                scale = lax.rsqrt(jnp.sum(value * value, axis=1, keepdims=True) + epsilon)
                scales[pl.ds(here, 16), :] = jnp.broadcast_to(scale, (16, 128))
                z[pl.ds(here, 16), :] = (value * scale).astype(BF16)
                return 0

            lax.fori_loop(0, rows // 16, chunk, 0, unroll=2)
            return 0

        lax.fori_loop(0, blocks, block, 0)

    for copy in copies_c:
        copy.wait()
    forward(xc, wc, raw_c, zc, sc_c, n_cap, rows)
    for copy in copies_i:
        copy.wait()
    forward(xi, wi, raw_i, zi, sc_i, n_img, img_rows)

    sharp, shift = factors[0], factors[1]
    spot = position[...]
    columns = n_cap * rows

    def back(source, offset, raw, scales, raw_offset, count, out):
        def chunk(r, _):
            here = pl.multiple_of(r * 16, 16)
            grad = source[pl.ds(pl.multiple_of(offset + here, 16), 16), :]
            there = pl.multiple_of(raw_offset + here, 16)
            scale = scales[pl.ds(there, 16), :][:, :1]
            unit = raw[pl.ds(there, 16), :] * scale
            along = jnp.sum(unit * grad, axis=1, keepdims=True)
            out[pl.ds(here, 16), :] = (scale * (grad - unit * along)).astype(out.dtype)
            return 0

        lax.fori_loop(0, count // 16, chunk, 0, unroll=2)

    for j in range(n_img):
        base = j * img_rows
        logits[...] = contract_last(zi[pl.ds(base, img_rows), :], zc[...])

        def chunk(r, _):
            here = pl.multiple_of(base + r * 16, 16)
            lo = first[pl.ds(here, 16), :]
            hi = last[pl.ds(here, 16), :]
            plus = weight[pl.ds(here, 16), :]
            for c in range(0, columns, 128):
                value = logits[pl.ds(pl.multiple_of(r * 16, 16), 16), pl.ds(c, 128)] * sharp + shift
                col = spot[:, c : c + 128]
                inside = (col >= lo) & (col < hi)
                power = jnp.exp(jnp.where(inside, value, -value))
                coef[pl.ds(here, 16), pl.ds(c, 128)] = (jnp.where(inside, plus, sharp) / (1.0 + power)).astype(BF16)
            return 0

        lax.fori_loop(0, img_rows // 16, chunk, 0)
        dz[...] = jnp.dot(coef[pl.ds(base, img_rows), :], zc[...], preferred_element_type=F32)
        if j < n_img - 1:
            back(dz, 0, raw_i, sc_i, base, img_rows, out_img_send.at[pl.ds(base, img_rows), :])
        else:
            back(dz, 0, raw_i, sc_i, base, img_rows, out_img_own)

    dzc[...] = contract_first(coef[...], zi[...])
    half = n_cap // 2
    back(dzc, 0, raw_c, sc_c, 0, half * rows, out_cap_core)
    if half > 1:
        back(dzc, half * rows, raw_c, sc_c, half * rows, (half - 1) * rows, out_cap_next)
    back(dzc, (n_cap - 1) * rows, raw_c, sc_c, (n_cap - 1) * rows, rows, out_cap_own)


def body(lay0, *args):
    img_x, cap_x, img_w, cap_w, counts, sharp, shift = args
    n_dp, slots = lax.axis_size("dp"), lax.axis_size("tensor")
    n_y = ROWS_Y
    n_x = n_dp // (n_y * CORES)
    rows = cap_x.shape[0]
    img_rows = img_x.shape[0]
    depth, width = cap_w.shape
    me = lax.axis_index("dp")
    mine = lax.axis_index("tensor")
    core = me % CORES
    pos_x = (me // CORES) % n_x
    pos_y = me // (CORES * n_x)

    def number(y, x, c):
        return (y * n_x + x) * CORES + c

    def from_y(value, k):
        pairs = [
            (number((y + k) % n_y, x, c), number(y, x, c))
            for y in range(n_y)
            for x in range(n_x)
            for c in range(CORES)
        ]
        return lax.ppermute(value, "dp", pairs)

    def from_x(value, k):
        pairs = [
            (number(y, (x + k) % n_x, c), number(y, x, c))
            for y in range(n_y)
            for x in range(n_x)
            for c in range(CORES)
        ]
        return lax.ppermute(value, "dp", pairs)

    def from_core(value):
        return lax.ppermute(value, "dp", [(s, s ^ 1) for s in range(n_dp)])

    def from_z(value, k):
        return lax.ppermute(value, "tensor", [((t + k) % slots, t) for t in range(slots)])

    cap_same = [cap_x] + [from_x(cap_x, k) for k in range(1, n_x)]
    cap_other = [from_core(block) for block in cap_same]
    img_all = [from_y(img_x, k) for k in range(1, n_y)] + [img_x]
    cap_all = cap_other + cap_same[1:] + cap_same[:1]

    def gathered(w, n_line, pos, from_line):
        n_p = n_line * CORES
        step = depth // n_p
        own = lax.dynamic_slice_in_dim(w, (pos * CORES + core) * step, step, axis=0)
        pieces = []
        for k in range(1, slots):
            piece = from_z(own, k)
            line = [piece] + [from_line(piece, j) for j in range(1, n_line)]
            pieces += line + [from_core(value) for value in line]
        where = [((pos + j) % n_line * CORES + core) * step for j in range(n_line)]
        where += [((pos + j) % n_line * CORES + (1 - core)) * step for j in range(n_line)]
        return pieces, where

    cap_pieces, cap_where = gathered(cap_w, n_x, pos_x, from_x)
    img_pieces, img_where = gathered(img_w, n_y, pos_y, from_y)
    n_pc, n_pi = n_x * CORES, n_y * CORES
    place = jnp.stack(cap_where + img_where).astype(jnp.int32)

    ends = jnp.cumsum(counts)
    starts = ends - counts

    def of_image(values):
        blocks = []
        for k in list(range(1, n_y)) + [0]:
            owner = number((pos_y + k) % n_y, pos_x, core)
            blocks.append(lax.dynamic_slice_in_dim(values, owner * img_rows, img_rows))
        return jnp.concatenate(blocks)[:, None]

    first = of_image(starts)
    last = of_image(ends)
    weight = -sharp[0] / of_image(counts).astype(F32)
    order = [(k, 1 - core) for k in range(n_x)] + [(k, core) for k in range(1, n_x)] + [(0, core)]
    position = jnp.concatenate(
        [
            (number(pos_y, (pos_x + k) % n_x, c) * slots + mine) * rows + jnp.arange(rows, dtype=jnp.int32)
            for k, c in order
        ]
    )[None, :]
    factors = jnp.concatenate([sharp, shift])

    n_cap, n_img = n_x * CORES, n_y
    lay = dict(n_cap=n_cap, n_img=n_img, rows=rows, img_rows=img_rows, n_pc=n_pc, n_pi=n_pi, slots=slots, width=width)
    full = slots * width
    n_copies = 2 + (slots - 1) * (n_pc + n_pi) + n_cap + n_img
    any_spec = pl.BlockSpec(memory_space=pl.ANY)
    vmem = pl.BlockSpec(memory_space=pltpu.VMEM)
    smem = pl.BlockSpec(memory_space=pltpu.SMEM)
    operands = [place] + cap_all + img_all + [cap_w] + cap_pieces + [img_w] + img_pieces
    specs = [smem] + [any_spec] * (len(operands) - 1) + [vmem] * 4 + [smem]
    operands += [first, last, weight, position, factors]
    next_rows = max(n_x - 1, 1) * rows
    products = n_cap * n_img * rows * img_rows * full * 6 + (n_cap * rows + n_img * img_rows) * depth * full * 2
    img_send, img_own, cap_core, cap_next, cap_own, wc, wi = pl.pallas_call(
        functools.partial(front_kernel, lay),
        out_shape=(
            jax.ShapeDtypeStruct(((n_y - 1) * img_rows, full), BF16),
            jax.ShapeDtypeStruct((img_rows, full), F32),
            jax.ShapeDtypeStruct((n_x * rows, full), BF16),
            jax.ShapeDtypeStruct((next_rows, full), F32),
            jax.ShapeDtypeStruct((rows, full), F32),
            jax.ShapeDtypeStruct((depth, full), BF16),
            jax.ShapeDtypeStruct((depth, full), BF16),
        ),
        in_specs=specs,
        out_specs=[vmem] * 7,
        scratch_shapes=[
            pltpu.VMEM((n_cap * rows, depth), BF16),
            pltpu.VMEM((n_img * img_rows, depth), BF16),
            pltpu.VMEM((n_cap * rows, full), BF16),
            pltpu.VMEM((n_img * img_rows, full), BF16),
            pltpu.VMEM((n_cap * rows, full), F32),
            pltpu.VMEM((n_img * img_rows, full), F32),
            pltpu.VMEM((n_cap * rows, 128), F32),
            pltpu.VMEM((n_img * img_rows, 128), F32),
            pltpu.VMEM((img_rows, n_cap * rows), F32),
            pltpu.VMEM((n_img * img_rows, n_cap * rows), BF16),
            pltpu.VMEM((img_rows, full), F32),
            pltpu.VMEM((n_cap * rows, full), F32),
            pltpu.SemaphoreType.DMA((n_copies,)),
        ],
        compiler_params=pltpu.CompilerParams(vmem_limit_bytes=60 * 2**20),
        cost_estimate=pl.CostEstimate(flops=products, bytes_accessed=20 * 2**20, transcendentals=0),
        name="front",
    )(*operands)

    img_total = img_own
    for k in range(1, n_y):
        sent = lax.slice_in_dim(img_send, (k - 1) * img_rows, k * img_rows)
        img_total = img_total + from_y(sent, n_y - k).astype(F32)
    img_part = contract_last(img_total.astype(BF16), wi)
    share = depth // slots

    def columns_of(k):
        return lax.dynamic_slice_in_dim(img_part, (mine + k) % slots * share, share, axis=1)

    grad_img = columns_of(0)
    for k in range(1, slots):
        grad_img = grad_img + from_z(columns_of(slots - k).astype(BF16), k).astype(F32)

    crossed = from_core(cap_core)
    cap_total = cap_own + crossed[:rows].astype(F32)
    for k in range(1, n_x):
        sent = cap_next[(k - 1) * rows : k * rows] + crossed[k * rows : (k + 1) * rows].astype(F32)
        cap_total = cap_total + from_x(sent.astype(BF16), n_x - k).astype(F32)
    grad_cap = contract_last(cap_total.astype(BF16), wc)
    return (grad_img.astype(BF16), grad_cap.astype(BF16))


def solution(mesh):
    in_specs = (
        P("dp", None),
        P(("dp", "tensor"), None),
        P(None, "tensor"),
        P(None, "tensor"),
        P(),
        P(),
        P(),
    )
    out_specs = (P("dp", "tensor"), P(("dp", "tensor"), None))
    return jax.shard_map(
        functools.partial(body, None), mesh=mesh, in_specs=in_specs, out_specs=out_specs, check_vma=False
    )
```

```python
import functools

import jax
import jax.numpy as jnp
from jax import lax
from jax.experimental import pallas as pl
from jax.experimental.pallas import tpu as pltpu
from jax.sharding import PartitionSpec as P


epsilon = 1e-06
CORES = 2
ROWS_Y = 2
CHUNK = 32
PARTS = 2
LOG2E = 1.4426950408889634
F32 = jnp.float32
BF16 = jnp.bfloat16


def contract_last(a, b):
    return lax.dot_general(a, b, (((1,), (1,)), ((), ())), preferred_element_type=F32)


def contract_first(a, b):
    return lax.dot_general(a, b, (((0,), (0,)), ((), ())), preferred_element_type=F32)


def lane_sums(partial):
    ones = jnp.ones((128, 128), BF16)
    upper = partial.astype(BF16)
    lower = (partial - upper.astype(F32)).astype(BF16)
    return jnp.dot(upper, ones, preferred_element_type=F32) + jnp.dot(lower, ones, preferred_element_type=F32)


def folded(pieces):
    while len(pieces) > 1:
        pieces = [pieces[n] + pieces[n + 1] for n in range(0, len(pieces) - 1, 2)] + (
            pieces[-1:] if len(pieces) % 2 else []
        )
    return pieces[0]


def cut(ref, row, lane, height=16):
    return ref[row : row + height, lane * 128 : lane * 128 + 128]


def forward(x, w, raw, z, scales, top, rows):
    lanes = w.shape[1] // 128
    raw[top : top + rows, :] = jnp.dot(x[top : top + rows, :], w[...], preferred_element_type=F32)
    for r in range(top, top + rows, 16):
        value = [cut(raw, r, n) for n in range(lanes)]
        scales[r : r + 16, :] = folded([v * v for v in value])
    scales[top : top + rows, :] = lax.rsqrt(lane_sums(scales[top : top + rows, :]) + epsilon)
    for r in range(top, top + rows, 16):
        scale = scales[r : r + 16, :]
        for n in range(lanes):
            z[r : r + 16, n * 128 : n * 128 + 128] = (cut(raw, r, n) * scale).astype(BF16)


def back(source, raw, scales, raw_offset, offset, count, out, along):
    lanes = source.shape[1] // 128
    for r in range(offset, offset + count, 16):
        there = raw_offset + r
        along[r : r + 16, :] = folded([cut(source, r, n) * cut(raw, there, n) for n in range(lanes)])
    along[offset : offset + count, :] = lane_sums(along[offset : offset + count, :])
    for r in range(offset, offset + count, 16):
        there = raw_offset + r
        scale = scales[there : there + 16, :]
        pull = along[r : r + 16, :] * (scale * scale * scale)
        for n in range(lanes):
            value = scale * cut(source, r, n) - pull * cut(raw, there, n)
            out[r - offset : r - offset + 16, n * 128 : n * 128 + 128] = value.astype(out.dtype)


class Copies:
    def __init__(self, sem):
        self.sem, self.used = sem, 0

    def start(self, src, dst):
        copy = pltpu.make_async_copy(src, dst, self.sem.at[self.used])
        self.used += 1
        copy.start()
        return copy


def wait_all(copies):
    for copy in copies:
        copy.wait()


def pair_kernel(lay, *refs):
    n_cap, n_img, n_pc, n_pi = lay["n_cap"], lay["n_img"], lay["n_pc"], lay["n_pi"]
    rows, img_rows = lay["rows"], lay["img_rows"]
    slots, width = lay["slots"], lay["width"]
    at = 0

    def take(count):
        nonlocal at
        got = refs[at : at + count]
        at += count
        return got

    (place,) = take(1)
    cap_x, img_x = take(n_cap), take(n_img)
    (wc_own,) = take(1)
    wc_pieces = take((slots - 1) * n_pc)
    (wi_own,) = take(1)
    wi_pieces = take((slots - 1) * n_pi)
    first, last, weight, position, factors = take(5)
    out_send = take((n_img - 1) * PARTS)
    out_coef, out_zc, out_zi, out_rc, out_ri, out_sc, out_si, out_wc, out_wi = take(9)
    xc, xi, zc, zi, raw_c, raw_i, sc_c, sc_i, wc, wi, logits, coef, dz, along, sem = take(15)

    depth = wc.shape[0]
    moves = Copies(sem)
    copies = {}
    for name, own, pieces, full, n_p, base in (
        ("c", wc_own, wc_pieces, wc, n_pc, 0),
        ("i", wi_own, wi_pieces, wi, n_pi, n_pc),
    ):
        step = depth // n_p
        copies[name] = [moves.start(own, full.at[:, pl.ds(0, width)])]
        for k in range(1, slots):
            for r in range(n_p):
                offset = pl.multiple_of(place[base + r], step)
                copies[name].append(
                    moves.start(
                        pieces[(k - 1) * n_p + r],
                        full.at[pl.ds(offset, step), pl.ds(k * width, width)],
                    )
                )
    for q in range(n_cap):
        copies["c"].append(moves.start(cap_x[q], xc.at[pl.ds(q * rows, rows), :]))
    for q in range(n_img):
        copies["i"].append(moves.start(img_x[q], xi.at[pl.ds(q * img_rows, img_rows), :]))

    outs = []
    wait_all(copies["c"])
    outs.append(moves.start(wc, out_wc))
    for q in range(n_cap):
        forward(xc, wc, raw_c, zc, sc_c, q * rows, rows)
    outs += [moves.start(raw_c, out_rc), moves.start(zc, out_zc), moves.start(sc_c, out_sc)]
    wait_all(copies["i"])
    outs.append(moves.start(wi, out_wi))
    for q in range(n_img):
        forward(xi, wi, raw_i, zi, sc_i, q * img_rows, img_rows)
    outs += [moves.start(raw_i, out_ri), moves.start(zi, out_zi), moves.start(sc_i, out_si)]

    sharp = factors[0]
    slope, level = -LOG2E * sharp, -LOG2E * factors[1]
    spot = position[...]
    columns = n_cap * rows
    part = img_rows // PARTS
    for j in range(n_img):
        base = j * img_rows
        logits[...] = contract_last(zi[pl.ds(base, img_rows), :], zc[...])

        def chunk(r, _):
            here = pl.multiple_of(base + r * CHUNK, 16)
            line = pl.ds(pl.multiple_of(r * CHUNK, 16), CHUNK)
            touched = place[n_pc + n_pi + j * (img_rows // CHUNK) + r] != 0

            @pl.when(touched)
            def _():
                lo = first[pl.ds(here, CHUNK), :]
                hi = last[pl.ds(here, CHUNK), :]
                plus = weight[pl.ds(here, CHUNK), :]
                for c in range(0, columns, 128):
                    value = logits[line, pl.ds(c, 128)] * slope + level
                    col = spot[:, c : c + 128]
                    inside = (col >= lo) & (col < hi)
                    power = jnp.exp2(jnp.where(inside, -value, value))
                    share = jnp.where(inside, plus, sharp) / (1.0 + power)
                    coef[pl.ds(here, CHUNK), pl.ds(c, 128)] = share.astype(BF16)

            @pl.when(jnp.logical_not(touched))
            def _():
                for c in range(0, columns, 128):
                    power = jnp.exp2(logits[line, pl.ds(c, 128)] * slope + level)
                    coef[pl.ds(here, CHUNK), pl.ds(c, 128)] = (sharp / (1.0 + power)).astype(BF16)

            return 0

        lax.fori_loop(0, img_rows // CHUNK, chunk, 0)
        outs.append(moves.start(coef.at[pl.ds(base, img_rows), :], out_coef.at[pl.ds(base, img_rows), :]))
        if j < n_img - 1:
            dz[...] = jnp.dot(coef[pl.ds(base, img_rows), :], zc[...], preferred_element_type=F32)
            for p in range(PARTS):
                back(dz, raw_i, sc_i, base, p * part, part, out_send[j * PARTS + p], along)
    wait_all(outs)


def caption_kernel(lay, coef_in, zi_in, rc_in, sc_in, out_core, out_next, out_own, coef, zi, raw, scales, dz, along, sem):
    n_cap, rows = lay["n_cap"], lay["rows"]
    moves = Copies(sem)
    early = [moves.start(coef_in, coef), moves.start(zi_in, zi)]
    late = [moves.start(rc_in, raw), moves.start(sc_in, scales)]
    wait_all(early)
    dz[...] = contract_first(coef[...], zi[...])
    wait_all(late)
    half = n_cap // 2
    back(dz, raw, scales, 0, 0, half * rows, out_core, along)
    if half > 1:
        back(dz, raw, scales, 0, half * rows, (half - 1) * rows, out_next, along)
    back(dz, raw, scales, 0, (n_cap - 1) * rows, rows, out_own, along)


def image_kernel(lay, coef_in, zc_in, ri_in, si_in, *refs):
    out_own, (coef, zc, raw, scales, dz, along, sem) = refs[:PARTS], refs[PARTS:]
    rows, top = lay["img_rows"], (lay["n_img"] - 1) * lay["img_rows"]
    part = pl.ds(top, rows)
    moves = Copies(sem)
    early = [moves.start(coef_in.at[part, :], coef), moves.start(zc_in, zc)]
    late = [moves.start(ri_in.at[part, :], raw), moves.start(si_in.at[part, :], scales)]
    wait_all(early)
    dz[...] = jnp.dot(coef[...], zc[...], preferred_element_type=F32)
    wait_all(late)
    for p in range(PARTS):
        back(dz, raw, scales, 0, p * (rows // PARTS), rows // PARTS, out_own[p], along)


def whole(*args):
    img_x, cap_x, img_w, cap_w, counts, sharp, shift = args
    n_dp, slots = lax.axis_size("dp"), lax.axis_size("tensor")
    n_y = ROWS_Y
    n_x = n_dp // (n_y * CORES)
    rows = cap_x.shape[0]
    img_rows = img_x.shape[0]
    depth, width = cap_w.shape
    me = lax.axis_index("dp")
    mine = lax.axis_index("tensor")
    core = me % CORES
    pos_x = (me // CORES) % n_x
    pos_y = me // (CORES * n_x)

    def number(y, x, c):
        return (y * n_x + x) * CORES + c

    def from_y(value, k):
        pairs = [
            (number((y + k) % n_y, x, c), number(y, x, c))
            for y in range(n_y)
            for x in range(n_x)
            for c in range(CORES)
        ]
        return lax.ppermute(value, "dp", pairs)

    def from_x(value, k):
        pairs = [
            (number(y, (x + k) % n_x, c), number(y, x, c))
            for y in range(n_y)
            for x in range(n_x)
            for c in range(CORES)
        ]
        return lax.ppermute(value, "dp", pairs)

    def from_core(value):
        return lax.ppermute(value, "dp", [(s, s ^ 1) for s in range(n_dp)])

    def from_z(value, k):
        return lax.ppermute(value, "tensor", [((t + k) % slots, t) for t in range(slots)])

    cap_same = [cap_x] + [from_x(cap_x, k) for k in range(1, n_x)]
    img_all = [from_y(img_x, k) for k in range(1, n_y)] + [img_x]
    cap_other = [from_core(block) for block in cap_same]
    cap_all = cap_other + cap_same[1:] + cap_same[:1]

    n_pc, n_pi = n_x * CORES, n_y * CORES
    step_c, step_i = depth // n_pc, depth // n_pi
    own = jnp.concatenate(
        [
            lax.dynamic_slice_in_dim(cap_w, (pos_x * CORES + core) * step_c, step_c, axis=0),
            lax.dynamic_slice_in_dim(img_w, (pos_y * CORES + core) * step_i, step_i, axis=0),
        ]
    )
    far = slots // 2
    got = {k: from_z(own, k) for k in range(1, slots) if k != far}
    own, _ = lax.optimization_barrier((own, tuple(got.values())))
    got[far] = from_z(own, far)

    cap_pieces, img_pieces = {}, {}
    for k in list(range(1, far)) + list(range(far + 1, slots)) + [far]:
        cap_line = [got[k][:step_c]]
        cap_line += [from_x(cap_line[0], j) for j in range(1, n_x)]
        img_line = [got[k][step_c:]]
        img_line += [from_y(img_line[0], j) for j in range(1, n_y)]
        cap_pieces[k] = cap_line + [from_core(value) for value in cap_line]
        img_pieces[k] = img_line + [from_core(value) for value in img_line]
    cap_pieces = [piece for k in range(1, slots) for piece in cap_pieces[k]]
    img_pieces = [piece for k in range(1, slots) for piece in img_pieces[k]]

    def places(n_line, pos, step):
        return [((pos + j) % n_line * CORES + c) * step for c in (core, 1 - core) for j in range(n_line)]

    place = jnp.stack(places(n_x, pos_x, step_c) + places(n_y, pos_y, step_i)).astype(jnp.int32)

    ends = jnp.cumsum(counts)
    starts = ends - counts

    def of_image(values):
        blocks = []
        for k in list(range(1, n_y)) + [0]:
            owner = number((pos_y + k) % n_y, pos_x, core)
            blocks.append(lax.dynamic_slice_in_dim(values, owner * img_rows, img_rows))
        return jnp.concatenate(blocks)[:, None]

    first = of_image(starts)
    last = of_image(ends)
    weight = -sharp[0] / of_image(counts).astype(F32)
    order = [(k, 1 - core) for k in range(n_x)] + [(k, core) for k in range(1, n_x)] + [(0, core)]
    heads = [(number(pos_y, (pos_x + k) % n_x, c) * slots + mine) * rows for k, c in order]
    position = jnp.concatenate([head + jnp.arange(rows, dtype=jnp.int32) for head in heads])[None, :]
    low, high = first[::CHUNK, 0], last[CHUNK - 1 :: CHUNK, 0]
    touched = functools.reduce(jnp.logical_or, [(low < head + rows) & (high > head) for head in heads])
    place = jnp.concatenate([place, touched.astype(jnp.int32)])
    factors = jnp.concatenate([sharp, shift])

    n_cap, n_img = n_x * CORES, n_y
    lay = dict(n_cap=n_cap, n_img=n_img, rows=rows, img_rows=img_rows, n_pc=n_pc, n_pi=n_pi, slots=slots, width=width)
    full = slots * width
    c_rows, i_rows = n_cap * rows, n_img * img_rows
    hbm = pl.BlockSpec(memory_space=pltpu.HBM)
    vmem = pl.BlockSpec(memory_space=pltpu.VMEM)
    smem = pl.BlockSpec(memory_space=pltpu.SMEM)

    def of(shape, dtype):
        return jax.ShapeDtypeStruct(shape, dtype)

    def params(mib):
        return pltpu.CompilerParams(vmem_limit_bytes=mib * 2**20)

    def cost(flops, mib):
        return pl.CostEstimate(flops=flops, bytes_accessed=mib * 2**20, transcendentals=0)

    pair = 2 * c_rows * i_rows * full
    operands = [place] + cap_all + img_all + [cap_w] + cap_pieces + [img_w] + img_pieces
    specs = [smem] + [hbm] * (len(operands) - 1) + [vmem] * 4 + [smem]
    operands += [first, last, weight, position, factors]
    n_copies = 2 + (slots - 1) * (n_pc + n_pi) + n_cap + n_img + 8 + n_img
    shared = (
        of((i_rows, c_rows), BF16),
        of((c_rows, full), BF16),
        of((i_rows, full), BF16),
        of((c_rows, full), F32),
        of((i_rows, full), F32),
        of((c_rows, 128), F32),
        of((i_rows, 128), F32),
        of((depth, full), BF16),
        of((depth, full), BF16),
    )
    half = img_rows // PARTS
    n_send = (n_y - 1) * PARTS
    made = pl.pallas_call(
        functools.partial(pair_kernel, lay),
        out_shape=tuple(of((half, full), BF16) for _ in range(n_send)) + shared,
        in_specs=specs,
        out_specs=[vmem] * n_send + [hbm] * len(shared),
        scratch_shapes=[
            pltpu.VMEM((c_rows, depth), BF16),
            pltpu.VMEM((i_rows, depth), BF16),
            pltpu.VMEM((c_rows, full), BF16),
            pltpu.VMEM((i_rows, full), BF16),
            pltpu.VMEM((c_rows, full), F32),
            pltpu.VMEM((i_rows, full), F32),
            pltpu.VMEM((c_rows, 128), F32),
            pltpu.VMEM((i_rows, 128), F32),
            pltpu.VMEM((depth, full), BF16),
            pltpu.VMEM((depth, full), BF16),
            pltpu.VMEM((img_rows, c_rows), F32),
            pltpu.VMEM((i_rows, c_rows), BF16),
            pltpu.VMEM((img_rows, full), F32),
            pltpu.VMEM((img_rows, 128), F32),
            pltpu.SemaphoreType.DMA((n_copies,)),
        ],
        compiler_params=params(60),
        cost_estimate=cost((c_rows + i_rows) * depth * full * 2 + pair * 3 // 2, 30),
        name="pairs",
    )(*operands)

    img_send = made[:n_send]
    coef, zc, zi, raw_c, raw_i, sc_c, sc_i, wc, wi = made[n_send:]

    img_sent = [
        [from_y(img_send[(k - 1) * PARTS + p], n_y - k) for k in range(1, n_y)] for p in range(PARTS)
    ]

    cap_core, cap_next, cap_own = pl.pallas_call(
        functools.partial(caption_kernel, lay),
        out_shape=(
            of((n_x * rows, full), BF16),
            of((max(n_x - 1, 1) * rows, full), F32),
            of((rows, full), F32),
        ),
        in_specs=[hbm] * 4,
        out_specs=[vmem] * 3,
        scratch_shapes=[
            pltpu.VMEM((i_rows, c_rows), BF16),
            pltpu.VMEM((i_rows, full), BF16),
            pltpu.VMEM((c_rows, full), F32),
            pltpu.VMEM((c_rows, 128), F32),
            pltpu.VMEM((c_rows, full), F32),
            pltpu.VMEM((c_rows, 128), F32),
            pltpu.SemaphoreType.DMA((4,)),
        ],
        compiler_params=params(60),
        cost_estimate=cost(pair, 20),
        name="captions",
    )(coef, zi, raw_c, sc_c)
    crossed = from_core(cap_core)

    img_own = pl.pallas_call(
        functools.partial(image_kernel, lay),
        out_shape=[of((half, full), F32)] * PARTS,
        in_specs=[hbm] * 4,
        out_specs=[vmem] * PARTS,
        scratch_shapes=[
            pltpu.VMEM((img_rows, c_rows), BF16),
            pltpu.VMEM((c_rows, full), BF16),
            pltpu.VMEM((img_rows, full), F32),
            pltpu.VMEM((img_rows, 128), F32),
            pltpu.VMEM((img_rows, full), F32),
            pltpu.VMEM((img_rows, 128), F32),
            pltpu.SemaphoreType.DMA((4,)),
        ],
        compiler_params=params(60),
        cost_estimate=cost(pair // n_img, 8),
        name="images",
    )(coef, zc, raw_i, sc_i)

    cap_total = cap_own + crossed[:rows].astype(F32)
    for k in range(1, n_x):
        sent = cap_next[(k - 1) * rows : k * rows] + crossed[k * rows : (k + 1) * rows].astype(F32)
        cap_total = cap_total + from_x(sent.astype(BF16), n_x - k).astype(F32)
    grad_cap = contract_last(cap_total.astype(BF16), wc).astype(BF16)

    share = depth // slots
    grad_img = []
    for p in range(PARTS):
        img_total = img_own[p]
        for arrived in img_sent[p]:
            img_total = img_total + arrived.astype(F32)
        img_part = contract_last(img_total.astype(BF16), wi)

        def columns_of(k):
            return lax.dynamic_slice_in_dim(img_part, (mine + k) % slots * share, share, axis=1)

        arrived = [from_z(columns_of(slots - k).astype(BF16), k) for k in range(1, slots)]
        grad_img.append(functools.reduce(lambda a, b: a + b.astype(F32), arrived, columns_of(0)).astype(BF16))
    return (jnp.concatenate(grad_img), grad_cap)


def solution(mesh):
    in_specs = (
        P("dp", None),
        P(("dp", "tensor"), None),
        P(None, "tensor"),
        P(None, "tensor"),
        P(),
        P(),
        P(),
    )
    out_specs = (P("dp", "tensor"), P(("dp", "tensor"), None))
    return jax.shard_map(whole, mesh=mesh, in_specs=in_specs, out_specs=out_specs, check_vma=False)
```

```python
import functools

import jax
import jax.numpy as jnp
from jax import lax
from jax.experimental import pallas as pl
from jax.experimental.pallas import tpu as pltpu
from jax.sharding import PartitionSpec as P


epsilon = 1e-06
CORES = 2
ROWS_Y = 2
CHUNK = 32
PARTS = 2
LOG2E = 1.4426950408889634
F32 = jnp.float32
BF16 = jnp.bfloat16


def contract_last(a, b):
    return lax.dot_general(a, b, (((1,), (1,)), ((), ())), preferred_element_type=F32)


def contract_first(a, b):
    return lax.dot_general(a, b, (((0,), (0,)), ((), ())), preferred_element_type=F32)


def split_rows(rows):
    units = rows // 16
    heights = [(units // PARTS + (n < units % PARTS)) * 16 for n in range(PARTS)]
    return [(sum(heights[:n]), heights[n]) for n in range(PARTS)]


def lane_sums(partial):
    ones = jnp.ones((128, 128), BF16)
    upper = partial.astype(BF16)
    lower = (partial - upper.astype(F32)).astype(BF16)
    return jnp.dot(upper, ones, preferred_element_type=F32) + jnp.dot(lower, ones, preferred_element_type=F32)


def folded(pieces):
    while len(pieces) > 1:
        pieces = [pieces[n] + pieces[n + 1] for n in range(0, len(pieces) - 1, 2)] + (
            pieces[-1:] if len(pieces) % 2 else []
        )
    return pieces[0]


def cut(ref, row, lane, height=16):
    return ref[row : row + height, lane * 128 : lane * 128 + 128]


def forward(x, w, raw, z, scales, top, rows):
    lanes = w.shape[1] // 128
    raw[top : top + rows, :] = jnp.dot(x[top : top + rows, :], w[...], preferred_element_type=F32)
    for r in range(top, top + rows, 16):
        value = [cut(raw, r, n) for n in range(lanes)]
        scales[r : r + 16, :] = folded([v * v for v in value])
    scales[top : top + rows, :] = lax.rsqrt(lane_sums(scales[top : top + rows, :]) + epsilon)
    for r in range(top, top + rows, 16):
        scale = scales[r : r + 16, :]
        for n in range(lanes):
            z[r : r + 16, n * 128 : n * 128 + 128] = (cut(raw, r, n) * scale).astype(BF16)


def back(source, raw, scales, raw_offset, offset, count, out, along):
    lanes = source.shape[1] // 128
    for r in range(offset, offset + count, 16):
        there = raw_offset + r
        along[r : r + 16, :] = folded([cut(source, r, n) * cut(raw, there, n) for n in range(lanes)])
    along[offset : offset + count, :] = lane_sums(along[offset : offset + count, :])
    for r in range(offset, offset + count, 16):
        there = raw_offset + r
        scale = scales[there : there + 16, :]
        pull = along[r : r + 16, :] * (scale * scale * scale)
        for n in range(lanes):
            value = scale * cut(source, r, n) - pull * cut(raw, there, n)
            out[r - offset : r - offset + 16, n * 128 : n * 128 + 128] = value.astype(out.dtype)


class Copies:
    def __init__(self, sem):
        self.sem, self.used = sem, 0

    def start(self, src, dst):
        copy = pltpu.make_async_copy(src, dst, self.sem.at[self.used])
        self.used += 1
        copy.start()
        return copy


def wait_all(copies):
    for copy in copies:
        copy.wait()


def place_weight(moves, own, pieces, groups, full, n_p, width, place, base):
    step = full.shape[0] // n_p
    copies = [moves.start(own, full.at[:, pl.ds(0, width)])]
    for g, group in enumerate(groups):
        for r in range(n_p):
            offset = pl.multiple_of(place[base + r], step)
            for n, k in enumerate(group):
                source = pieces[g * n_p + r].at[pl.ds(n * step, step), :]
                copies.append(moves.start(source, full.at[pl.ds(offset, step), pl.ds(k * width, width)]))
    return copies


class Operands:
    def __init__(self, refs):
        self.refs = list(refs)

    def take(self, count):
        got, self.refs = self.refs[:count], self.refs[count:]
        return got

    def one(self):
        return self.take(1)[0]


def pair_kernel(lay, *refs):
    n_cap, n_img, n_pc, n_pi = lay["n_cap"], lay["n_img"], lay["n_pc"], lay["n_pi"]
    rows, img_rows = lay["rows"], lay["img_rows"]
    groups, width = lay["groups"], lay["width"]
    args = Operands(refs)
    place, cap_x, img_x = args.one(), args.take(n_cap), args.take(n_img)
    own_c, pieces_c = args.one(), args.take(len(groups) * n_pc)
    own_i, pieces_i = args.one(), args.take(len(groups) * n_pi)
    first, last, weight, position, factors = args.take(5)
    out_img = args.take(n_img * PARTS)
    out_coef, out_zi, out_rc, out_sc, out_wc, out_wi = args.take(6)
    xc, xi, zc, zi, raw_c, raw, sc_c, scales, wc, wi, logits, coef, dz, along, sem = args.take(15)

    moves = Copies(sem)
    heads_c = place_weight(moves, own_c, pieces_c, groups, wc, n_pc, width, place, 0)
    features_c = [moves.start(cap_x[q], xc.at[pl.ds(q * rows, rows), :]) for q in range(n_cap)]
    heads_i = place_weight(moves, own_i, pieces_i, groups, wi, n_pi, width, place, n_pc)
    features_i = [moves.start(img_x[q], xi.at[pl.ds(q * img_rows, img_rows), :]) for q in range(n_img)]
    wait_all(heads_c)
    outs = [moves.start(wc, out_wc)]
    for q in range(n_cap):
        features_c[q].wait()
        forward(xc, wc, raw_c, zc, sc_c, q * rows, rows)
        here = pl.ds(q * rows, rows)
        outs.append(moves.start(raw_c.at[here, :], out_rc.at[here, :]))
    outs.append(moves.start(sc_c, out_sc))
    wait_all(heads_i)
    outs.append(moves.start(wi, out_wi))
    for q in range(n_img):
        features_i[q].wait()
        forward(xi, wi, raw, zi, scales, q * img_rows, img_rows)
    outs.append(moves.start(zi, out_zi))

    sharp = factors[0]
    slope, level = -LOG2E * sharp, -LOG2E * factors[1]
    spot = position[...]
    columns = n_cap * rows
    for j in range(n_img):
        base = j * img_rows
        logits[...] = contract_last(zi[pl.ds(base, img_rows), :], zc[...])

        def chunk(r, _):
            here = pl.multiple_of(base + r * CHUNK, 16)
            line = pl.ds(pl.multiple_of(r * CHUNK, 16), CHUNK)
            touched = place[n_pc + n_pi + j * (img_rows // CHUNK) + r] != 0

            @pl.when(touched)
            def _():
                lo = first[pl.ds(here, CHUNK), :]
                hi = last[pl.ds(here, CHUNK), :]
                plus = weight[pl.ds(here, CHUNK), :]
                for c in range(0, columns, 128):
                    value = logits[line, pl.ds(c, 128)] * slope + level
                    col = spot[:, c : c + 128]
                    inside = (col >= lo) & (col < hi)
                    power = jnp.exp2(jnp.where(inside, -value, value))
                    share = jnp.where(inside, plus, sharp) / (1.0 + power)
                    coef[pl.ds(here, CHUNK), pl.ds(c, 128)] = share.astype(BF16)

            @pl.when(jnp.logical_not(touched))
            def _():
                for c in range(0, columns, 128):
                    power = jnp.exp2(logits[line, pl.ds(c, 128)] * slope + level)
                    coef[pl.ds(here, CHUNK), pl.ds(c, 128)] = (sharp / (1.0 + power)).astype(BF16)

            return 0

        lax.fori_loop(0, img_rows // CHUNK, chunk, 0)
        outs.append(moves.start(coef.at[pl.ds(base, img_rows), :], out_coef.at[pl.ds(base, img_rows), :]))
        dz[...] = jnp.dot(coef[pl.ds(base, img_rows), :], zc[...], preferred_element_type=F32)
        for p, (top, height) in enumerate(split_rows(img_rows)):
            back(dz, raw, scales, base, top, height, out_img[j * PARTS + p], along)
    wait_all(outs)


def caption_kernel(span, heights, coef_in, zi_in, rc_in, sc_in, *refs):
    results, (coef, zi, raw, scales, dz, along), sums, sem = refs[:2], refs[2:8], refs[8:10], refs[10]
    low, high, top = span
    moves = Copies(sem)
    early = [moves.start(zi_in, zi), moves.start(coef_in.at[:, pl.ds(low, high - low)], coef)]
    late = [moves.start(sc_in.at[pl.ds(low, high - low), :], scales), moves.start(rc_in.at[pl.ds(low, high - low), :], raw)]
    wait_all(early)
    dz[...] = contract_first(coef[...], zi[...])
    wait_all(late)
    outs, offset = [], top - low
    for n, height in enumerate(heights):
        back(dz, raw, scales, 0, offset, height, sums[n], along)
        outs.append(moves.start(sums[n], results[n]))
        offset += height
    wait_all(outs)


def whole(*args):
    img_x, cap_x, img_w, cap_w, counts, sharp, shift = args
    n_dp, slots = lax.axis_size("dp"), lax.axis_size("tensor")
    n_y = ROWS_Y
    n_x = n_dp // (n_y * CORES)
    rows = cap_x.shape[0]
    img_rows = img_x.shape[0]
    depth, width = cap_w.shape
    me = lax.axis_index("dp")
    mine = lax.axis_index("tensor")
    core = me % CORES
    pos_x = (me // CORES) % n_x
    pos_y = me // (CORES * n_x)

    def number(y, x, c):
        return (y * n_x + x) * CORES + c

    def from_y(value, k):
        pairs = [
            (number((y + k) % n_y, x, c), number(y, x, c))
            for y in range(n_y)
            for x in range(n_x)
            for c in range(CORES)
        ]
        return lax.ppermute(value, "dp", pairs)

    def from_x(value, k):
        pairs = [
            (number(y, (x + k) % n_x, c), number(y, x, c))
            for y in range(n_y)
            for x in range(n_x)
            for c in range(CORES)
        ]
        return lax.ppermute(value, "dp", pairs)

    def from_core(value):
        return lax.ppermute(value, "dp", [(s, s ^ 1) for s in range(n_dp)])

    def from_z(value, k):
        return lax.ppermute(value, "tensor", [((t + k) % slots, t) for t in range(slots)])

    cap_same = [cap_x] + [from_x(cap_x, k) for k in range(1, n_x)]
    img_all = [from_y(img_x, k) for k in range(1, n_y)] + [img_x]
    cap_other = [from_core(block) for block in cap_same]
    cap_all = cap_other[1:] + cap_same[1:] + cap_other[:1] + cap_same[:1]

    n_pc, n_pi = n_x * CORES, n_y * CORES
    step_c, step_i = depth // n_pc, depth // n_pi

    def places(n_line, pos, step):
        return [((pos + j) % n_line * CORES + c) * step for c in (core, 1 - core) for j in range(n_line)]

    place = jnp.stack(places(n_x, pos_x, step_c) + places(n_y, pos_y, step_i)).astype(jnp.int32)

    ends = jnp.cumsum(counts)
    starts = ends - counts

    def of_image(values):
        blocks = []
        for k in list(range(1, n_y)) + [0]:
            owner = number((pos_y + k) % n_y, pos_x, core)
            blocks.append(lax.dynamic_slice_in_dim(values, owner * img_rows, img_rows))
        return jnp.concatenate(blocks)[:, None]

    first = of_image(starts)
    last = of_image(ends)
    weight = -sharp[0] / of_image(counts).astype(F32)
    order = [(k, c) for c in (1 - core, core) for k in range(1, n_x)] + [(0, 1 - core), (0, core)]
    heads = [(number(pos_y, (pos_x + k) % n_x, c) * slots + mine) * rows for k, c in order]
    position = jnp.concatenate([head + jnp.arange(rows, dtype=jnp.int32) for head in heads])[None, :]
    low, high = first[::CHUNK, 0], last[CHUNK - 1 :: CHUNK, 0]
    touched = functools.reduce(jnp.logical_or, [(low < head + rows) & (high > head) for head in heads])
    place = jnp.concatenate([place, touched.astype(jnp.int32)])
    factors = jnp.concatenate([sharp, shift])

    far = slots // 2
    near = [k for n in range(1, far) for k in (n, slots - n)]
    groups = [near, [far]]
    own = jnp.concatenate(
        [
            lax.dynamic_slice_in_dim(cap_w, (pos_x * CORES + core) * step_c, step_c, axis=0),
            lax.dynamic_slice_in_dim(img_w, (pos_y * CORES + core) * step_i, step_i, axis=0),
        ]
    )
    slices = {k: from_z(own, k) for k in near}
    tables = (place, first, last, weight, position)
    own, _, tables = lax.optimization_barrier((own, tuple(slices.values()), tables))
    place, first, last, weight, position = tables
    slices[far] = from_z(own, far)

    cap_pieces, img_pieces = [], []
    for group in groups:
        cap_line = [jnp.concatenate([slices[k][:step_c] for k in group])]
        img_line = [jnp.concatenate([slices[k][step_c:] for k in group])]
        cap_line += [from_x(cap_line[0], j) for j in range(1, n_x)]
        img_line += [from_y(img_line[0], j) for j in range(1, n_y)]
        cap_pieces += cap_line + [from_core(value) for value in cap_line]
        img_pieces += img_line + [from_core(value) for value in img_line]

    n_cap, n_img = n_x * CORES, n_y
    lay = dict(n_cap=n_cap, n_img=n_img, rows=rows, img_rows=img_rows, n_pc=n_pc, n_pi=n_pi, width=width)
    lay.update(groups=groups)
    full = slots * width
    c_rows, i_rows = n_cap * rows, n_img * img_rows
    hbm = pl.BlockSpec(memory_space=pltpu.HBM)
    vmem = pl.BlockSpec(memory_space=pltpu.VMEM)
    smem = pl.BlockSpec(memory_space=pltpu.SMEM)

    def of(shape, dtype):
        return jax.ShapeDtypeStruct(shape, dtype)

    def params(mib):
        return pltpu.CompilerParams(vmem_limit_bytes=mib * 2**20)

    def cost(flops, mib):
        return pl.CostEstimate(flops=flops, bytes_accessed=mib * 2**20, transcendentals=0)

    pair = 2 * c_rows * i_rows * full
    heights = [height for _, height in split_rows(img_rows)]
    n_out = n_img * PARTS
    n_copies = 2 + (slots - 1) * (n_pc + n_pi) + 2 * n_cap + 2 * n_img + 4
    operands = [place] + cap_all + img_all + [cap_w] + cap_pieces + [img_w] + img_pieces
    specs = [smem] + [hbm] * (len(operands) - 1) + [vmem] * 4 + [smem]
    operands += [first, last, weight, position, factors]
    n_send = (n_img - 1) * PARTS
    made = pl.pallas_call(
        functools.partial(pair_kernel, lay),
        out_shape=tuple(of((heights[n % PARTS], full), BF16 if n < n_send else F32) for n in range(n_out))
        + (
            of((i_rows, c_rows), BF16),
            of((i_rows, full), BF16),
            of((c_rows, full), F32),
            of((c_rows, 128), F32),
            of((depth, full), BF16),
            of((depth, full), BF16),
        ),
        in_specs=specs,
        out_specs=[vmem] * n_out + [hbm] * 6,
        scratch_shapes=[
            pltpu.VMEM((c_rows, depth), BF16),
            pltpu.VMEM((i_rows, depth), BF16),
            pltpu.VMEM((c_rows, full), BF16),
            pltpu.VMEM((i_rows, full), BF16),
            pltpu.VMEM((c_rows, full), F32),
            pltpu.VMEM((i_rows, full), F32),
            pltpu.VMEM((c_rows, 128), F32),
            pltpu.VMEM((i_rows, 128), F32),
            pltpu.VMEM((depth, full), BF16),
            pltpu.VMEM((depth, full), BF16),
            pltpu.VMEM((img_rows, c_rows), F32),
            pltpu.VMEM((i_rows, c_rows), BF16),
            pltpu.VMEM((img_rows, full), F32),
            pltpu.VMEM((img_rows, 128), F32),
            pltpu.SemaphoreType.DMA((n_copies,)),
        ],
        compiler_params=params(60),
        cost_estimate=cost((c_rows + i_rows) * depth * full * 2 + 2 * pair, 20),
        name="pairs",
    )(*operands)
    img_send, img_own = made[:n_send], made[n_send:n_out]
    coef, zi, raw_c, sc_c, wc, wi = made[n_out:]

    img_sent = []
    for p in range(PARTS):
        parts = [img_send[(k - 1) * PARTS + p] for k in range(1, n_y)]
        img_sent.append([from_y(parts[k - 1], n_y - k) for k in range(1, n_y)])

    def caption_sums(top, heights):
        low = top // 128 * 128
        high = min(-(-(top + sum(heights)) // 128) * 128, c_rows)
        span = high - low
        return pl.pallas_call(
            functools.partial(caption_kernel, (low, high, top), heights),
            out_shape=(of((heights[0], full), BF16), of((heights[1], full), F32)),
            in_specs=[hbm] * 4,
            out_specs=[hbm] * 2,
            scratch_shapes=[
                pltpu.VMEM((i_rows, span), BF16),
                pltpu.VMEM((i_rows, full), BF16),
                pltpu.VMEM((span, full), F32),
                pltpu.VMEM((span, 128), F32),
                pltpu.VMEM((span, full), F32),
                pltpu.VMEM((span, 128), F32),
                pltpu.VMEM((heights[0], full), BF16),
                pltpu.VMEM((heights[1], full), F32),
                pltpu.SemaphoreType.DMA((6,)),
            ],
            compiler_params=params(60),
            cost_estimate=cost(2 * span * i_rows * full, 10),
            name="captions",
        )(coef, zi, raw_c, sc_c)

    others = (n_x - 1) * rows
    arrived = []
    if others:
        to_core, to_next = caption_sums(0, (others, others))
        crossed = from_core(to_core)
        for k in range(1, n_x):
            here = slice((k - 1) * rows, k * rows)
            sent = (to_next[here] + crossed[here].astype(F32)).astype(BF16)
            arrived.append(from_x(sent, n_x - k))
    to_core, cap_own = caption_sums(2 * others, (rows, rows))
    crossed = from_core(to_core)
    cap_total = functools.reduce(lambda a, b: a + b.astype(F32), arrived, cap_own + crossed.astype(F32))
    grad_cap = contract_last(cap_total.astype(BF16), wc).astype(BF16)

    share = depth // slots
    grad_img = []
    for p in range(PARTS):
        img_total = img_own[p]
        for arrived in img_sent[p]:
            img_total = img_total + arrived.astype(F32)
        img_part = contract_last(img_total.astype(BF16), wi)

        def columns_of(k):
            return lax.dynamic_slice_in_dim(img_part, (mine + k) % slots * share, share, axis=1)

        arrived = [from_z(columns_of(slots - k).astype(BF16), k) for k in range(1, slots)]
        grad_img.append(functools.reduce(lambda a, b: a + b.astype(F32), arrived, columns_of(0)).astype(BF16))
    return (jnp.concatenate(grad_img), grad_cap)


def solution(mesh):
    in_specs = (
        P("dp", None),
        P(("dp", "tensor"), None),
        P(None, "tensor"),
        P(None, "tensor"),
        P(),
        P(),
        P(),
    )
    out_specs = (P("dp", "tensor"), P(("dp", "tensor"), None))
    return jax.shard_map(whole, mesh=mesh, in_specs=in_specs, out_specs=out_specs, check_vma=False)
```

```python
import functools

import jax
import jax.numpy as jnp
from jax import lax
from jax.experimental import pallas as pl
from jax.experimental.pallas import tpu as pltpu
from jax.sharding import PartitionSpec as P


epsilon = 1e-06
CORES = 2
ROWS_Y = 2
CHUNK = 32
PARTS = 2
LOG2E = 1.4426950408889634
F32 = jnp.float32
BF16 = jnp.bfloat16


def contract_last(a, b):
    return lax.dot_general(a, b, (((1,), (1,)), ((), ())), preferred_element_type=F32)


def contract_first(a, b):
    return lax.dot_general(a, b, (((0,), (0,)), ((), ())), preferred_element_type=F32)


def split_rows(rows):
    units = rows // 16
    heights = [(units // PARTS + (n < units % PARTS)) * 16 for n in range(PARTS)]
    return [(sum(heights[:n]), heights[n]) for n in range(PARTS)]


def lane_sums(partial):
    ones = jnp.ones((128, 128), BF16)
    upper = partial.astype(BF16)
    lower = (partial - upper.astype(F32)).astype(BF16)
    return jnp.dot(upper, ones, preferred_element_type=F32) + jnp.dot(lower, ones, preferred_element_type=F32)


def folded(pieces):
    while len(pieces) > 1:
        pieces = [pieces[n] + pieces[n + 1] for n in range(0, len(pieces) - 1, 2)] + (
            pieces[-1:] if len(pieces) % 2 else []
        )
    return pieces[0]


def cut(ref, row, lane, height=16):
    return ref[row : row + height, lane * 128 : lane * 128 + 128]


def forward(x, w, raw, z, scales, top, rows):
    lanes = w.shape[1] // 128
    raw[top : top + rows, :] = jnp.dot(x[top : top + rows, :], w[...], preferred_element_type=F32)
    for r in range(top, top + rows, 16):
        value = [cut(raw, r, n) for n in range(lanes)]
        scales[r : r + 16, :] = folded([v * v for v in value])
    scales[top : top + rows, :] = lax.rsqrt(lane_sums(scales[top : top + rows, :]) + epsilon)
    for r in range(top, top + rows, 16):
        scale = scales[r : r + 16, :]
        for n in range(lanes):
            z[r : r + 16, n * 128 : n * 128 + 128] = (cut(raw, r, n) * scale).astype(BF16)


def back(source, raw, scales, raw_offset, offset, count, out, along):
    lanes = source.shape[1] // 128
    for r in range(offset, offset + count, 16):
        there = raw_offset + r
        along[r : r + 16, :] = folded([cut(source, r, n) * cut(raw, there, n) for n in range(lanes)])
    along[offset : offset + count, :] = lane_sums(along[offset : offset + count, :])
    for r in range(offset, offset + count, 16):
        there = raw_offset + r
        scale = scales[there : there + 16, :]
        pull = along[r : r + 16, :] * (scale * scale * scale)
        for n in range(lanes):
            value = scale * cut(source, r, n) - pull * cut(raw, there, n)
            out[r - offset : r - offset + 16, n * 128 : n * 128 + 128] = value.astype(out.dtype)


class Copies:
    def __init__(self, sem):
        self.sem, self.used = sem, 0

    def start(self, src, dst):
        copy = pltpu.make_async_copy(src, dst, self.sem.at[self.used])
        self.used += 1
        copy.start()
        return copy


def wait_all(copies):
    for copy in copies:
        copy.wait()


def place_weight(moves, own, pieces, groups, full, n_p, width, place, base):
    step = full.shape[0] // n_p
    copies = [moves.start(own, full.at[:, pl.ds(0, width)])]
    for g, group in enumerate(groups):
        for r in range(n_p):
            offset = pl.multiple_of(place[base + r], step)
            for n, k in enumerate(group):
                source = pieces[g * n_p + r].at[pl.ds(n * step, step), :]
                copies.append(moves.start(source, full.at[pl.ds(offset, step), pl.ds(k * width, width)]))
    return copies


class Operands:
    def __init__(self, refs):
        self.refs = list(refs)

    def take(self, count):
        got, self.refs = self.refs[:count], self.refs[count:]
        return got

    def one(self):
        return self.take(1)[0]


def pair_kernel(lay, *refs):
    n_cap, n_img, n_pc, n_pi = lay["n_cap"], lay["n_img"], lay["n_pc"], lay["n_pi"]
    rows, img_rows = lay["rows"], lay["img_rows"]
    groups, width = lay["groups"], lay["width"]
    args = Operands(refs)
    place, cap_x, img_x = args.one(), args.take(n_cap), args.take(n_img)
    head_c, pieces_c = args.one(), args.take(len(groups) * n_pc)
    head_i, pieces_i = args.one(), args.take(len(groups) * n_pi)
    table, position, factors = args.take(3)
    out_img = args.take(n_img * PARTS)
    out_core, out_next, out_own, out_wc, out_wi = args.take(5)
    xc, xi, zc, zi, raw_c, raw, sc_c, scales, wc, wi, bounds, logits, coef, dz, dzc, along = args.take(16)
    img_sums = args.take(n_img * PARTS)
    to_core, to_next, own, sem = args.take(4)

    moves = Copies(sem)
    heads_c = place_weight(moves, head_c, pieces_c, groups, wc, n_pc, width, place, 0)
    features_c = [moves.start(cap_x[q], xc.at[pl.ds(q * rows, rows), :]) for q in range(n_cap)]
    heads_i = place_weight(moves, head_i, pieces_i, groups, wi, n_pi, width, place, n_pc)
    features_i = [moves.start(img_x[q], xi.at[pl.ds(q * img_rows, img_rows), :]) for q in range(n_img)]
    wait_all(heads_c)
    outs = [moves.start(wc, out_wc)]
    for q in range(n_cap):
        features_c[q].wait()
        forward(xc, wc, raw_c, zc, sc_c, q * rows, rows)
    wait_all(heads_i)
    outs.append(moves.start(wi, out_wi))
    for q in range(n_img):
        features_i[q].wait()
        forward(xi, wi, raw, zi, scales, q * img_rows, img_rows)

    sharp = factors[0]
    slope, level = -LOG2E * sharp, -LOG2E * factors[1]
    spot = position[...]
    bounds[...] = jnp.transpose(table[...])
    columns = n_cap * rows
    for j in range(n_img):
        base = j * img_rows
        logits[...] = contract_last(zi[pl.ds(base, img_rows), :], zc[...])

        def chunk(r, _):
            here = pl.multiple_of(base + r * CHUNK, 16)
            line = pl.ds(pl.multiple_of(r * CHUNK, 16), CHUNK)
            touched = place[n_pc + n_pi + j * (img_rows // CHUNK) + r] != 0

            @pl.when(touched)
            def _():
                bound = bounds[pl.ds(here, CHUNK), :]
                lo, hi, plus = bound[:, 0:1], bound[:, 1:2], bound[:, 2:3]
                for c in range(0, columns, 128):
                    value = logits[line, pl.ds(c, 128)] * slope + level
                    col = spot[:, c : c + 128]
                    inside = (col >= lo) & (col < hi)
                    power = jnp.exp2(jnp.where(inside, -value, value))
                    share = jnp.where(inside, plus, sharp) / (1.0 + power)
                    coef[pl.ds(here, CHUNK), pl.ds(c, 128)] = share.astype(BF16)

            @pl.when(jnp.logical_not(touched))
            def _():
                for c in range(0, columns, 128):
                    power = jnp.exp2(logits[line, pl.ds(c, 128)] * slope + level)
                    coef[pl.ds(here, CHUNK), pl.ds(c, 128)] = (sharp / (1.0 + power)).astype(BF16)

            return 0

        lax.fori_loop(0, img_rows // CHUNK, chunk, 0)
        if j == n_img - 1:
            dzc[...] = contract_first(coef[...], zi[...])
            others = (n_cap // 2 - 1) * rows
            back(dzc, raw_c, sc_c, 0, 0, others, to_core.at[pl.ds(0, others), :], along)
            back(dzc, raw_c, sc_c, 0, 2 * others, rows, to_core.at[pl.ds(others, rows), :], along)
            outs.append(moves.start(to_core, out_core))
            if others:
                back(dzc, raw_c, sc_c, 0, others, others, to_next, along)
                outs.append(moves.start(to_next, out_next))
            back(dzc, raw_c, sc_c, 0, 2 * others + rows, rows, own, along)
            outs.append(moves.start(own, out_own))
        dz[...] = jnp.dot(coef[pl.ds(base, img_rows), :], zc[...], preferred_element_type=F32)
        for p, (top, height) in enumerate(split_rows(img_rows)):
            n = j * PARTS + p
            back(dz, raw, scales, base, top, height, img_sums[n], along)
            outs.append(moves.start(img_sums[n], out_img[n]))
    wait_all(outs)


def whole(*args):
    img_x, cap_x, img_w, cap_w, counts, sharp, shift = args
    n_dp, slots = lax.axis_size("dp"), lax.axis_size("tensor")
    n_y = ROWS_Y
    n_x = n_dp // (n_y * CORES)
    rows = cap_x.shape[0]
    img_rows = img_x.shape[0]
    depth, width = cap_w.shape
    me = lax.axis_index("dp")
    mine = lax.axis_index("tensor")
    core = me % CORES
    pos_x = (me // CORES) % n_x
    pos_y = me // (CORES * n_x)

    def number(y, x, c):
        return (y * n_x + x) * CORES + c

    def from_y(value, k):
        pairs = [
            (number((y + k) % n_y, x, c), number(y, x, c))
            for y in range(n_y)
            for x in range(n_x)
            for c in range(CORES)
        ]
        return lax.ppermute(value, "dp", pairs)

    def from_x(value, k):
        pairs = [
            (number(y, (x + k) % n_x, c), number(y, x, c))
            for y in range(n_y)
            for x in range(n_x)
            for c in range(CORES)
        ]
        return lax.ppermute(value, "dp", pairs)

    def from_core(value):
        return lax.ppermute(value, "dp", [(s, s ^ 1) for s in range(n_dp)])

    def from_z(value, k):
        return lax.ppermute(value, "tensor", [((t + k) % slots, t) for t in range(slots)])

    cap_same = [cap_x] + [from_x(cap_x, k) for k in range(1, n_x)]
    img_all = [from_y(img_x, k) for k in range(1, n_y)] + [img_x]
    cap_other = [from_core(block) for block in cap_same]
    cap_all = cap_other[1:] + cap_same[1:] + cap_other[:1] + cap_same[:1]

    n_pc, n_pi = n_x * CORES, n_y * CORES
    step_c, step_i = depth // n_pc, depth // n_pi

    def places(n_line, pos, step):
        return [((pos + j) % n_line * CORES + c) * step for c in (core, 1 - core) for j in range(n_line)]

    place = jnp.stack(places(n_x, pos_x, step_c) + places(n_y, pos_y, step_i)).astype(jnp.int32)

    ends = jnp.cumsum(counts)
    starts = ends - counts

    weights = -sharp[0] / counts.astype(F32)
    limits = jnp.stack([starts.astype(F32), ends.astype(F32), weights] + [weights] * 5)
    n_rows = n_y * img_rows
    padded = -(-n_rows // 128) * 128
    near_y = [number((pos_y + k) % n_y, pos_x, core) for k in list(range(1, n_y)) + [0]]
    table = jnp.concatenate(
        [lax.dynamic_slice_in_dim(limits, owner * img_rows, img_rows, axis=1) for owner in near_y]
        + ([jnp.zeros((8, padded - n_rows), F32)] if padded > n_rows else []),
        axis=1,
    )
    order = [(k, c) for c in (1 - core, core) for k in range(1, n_x)] + [(0, 1 - core), (0, core)]
    heads = [(number(pos_y, (pos_x + k) % n_x, c) * slots + mine) * rows for k, c in order]
    position = jnp.concatenate([head + jnp.arange(rows, dtype=jnp.int32) for head in heads]).astype(F32)[None, :]
    low = table[0, :n_rows].reshape(-1, CHUNK)[:, 0]
    high = table[1, :n_rows].reshape(-1, CHUNK)[:, -1]
    touched = functools.reduce(jnp.logical_or, [(low < head + rows) & (high > head) for head in heads])
    place = jnp.concatenate([place, touched.astype(jnp.int32)])
    factors = jnp.concatenate([sharp, shift])

    far = slots // 2
    near = [k for n in range(1, far) for k in (n, slots - n)]
    groups = [near, [far]]
    own = jnp.concatenate(
        [
            lax.dynamic_slice_in_dim(cap_w, (pos_x * CORES + core) * step_c, step_c, axis=0),
            lax.dynamic_slice_in_dim(img_w, (pos_y * CORES + core) * step_i, step_i, axis=0),
        ]
    )
    slices = {k: from_z(own, k) for k in near}
    tables = (place, table, position, factors)
    own, _, tables = lax.optimization_barrier((own, tuple(slices.values()), tables))
    place, table, position, factors = tables
    slices[far] = from_z(own, far)

    cap_pieces, img_pieces = [], []
    for group in groups:
        cap_line = [jnp.concatenate([slices[k][:step_c] for k in group])]
        img_line = [jnp.concatenate([slices[k][step_c:] for k in group])]
        cap_line += [from_x(cap_line[0], j) for j in range(1, n_x)]
        img_line += [from_y(img_line[0], j) for j in range(1, n_y)]
        cap_pieces += cap_line + [from_core(value) for value in cap_line]
        img_pieces += img_line + [from_core(value) for value in img_line]

    n_cap, n_img = n_x * CORES, n_y
    lay = dict(n_cap=n_cap, n_img=n_img, rows=rows, img_rows=img_rows, n_pc=n_pc, n_pi=n_pi, width=width)
    lay.update(groups=groups)
    full = slots * width
    c_rows, i_rows = n_cap * rows, n_img * img_rows
    hbm = pl.BlockSpec(memory_space=pltpu.HBM)
    vmem = pl.BlockSpec(memory_space=pltpu.VMEM)
    smem = pl.BlockSpec(memory_space=pltpu.SMEM)

    def of(shape, dtype):
        return jax.ShapeDtypeStruct(shape, dtype)

    def params(mib):
        return pltpu.CompilerParams(vmem_limit_bytes=mib * 2**20)

    def cost(flops, mib):
        return pl.CostEstimate(flops=flops, bytes_accessed=mib * 2**20, transcendentals=0)

    pair = 2 * c_rows * i_rows * full
    heights = [height for _, height in split_rows(img_rows)]
    n_out = n_img * PARTS
    n_copies = 2 + (slots - 1) * (n_pc + n_pi) + n_cap + n_img + n_img * PARTS + 5
    operands = [place] + cap_all + img_all + [cap_w] + cap_pieces + [img_w] + img_pieces
    specs = [smem] + [hbm] * (len(operands) - 1) + [vmem] * 2 + [smem]
    operands += [table, position, factors]
    n_send = (n_img - 1) * PARTS
    others = (n_x - 1) * rows
    results = [((heights[n % PARTS], full), BF16 if n < n_send else F32) for n in range(n_out)]
    results += [((n_x * rows, full), BF16), ((max(others, 16), full), F32), ((rows, full), F32)]
    made = pl.pallas_call(
        functools.partial(pair_kernel, lay),
        out_shape=tuple(of(*kind) for kind in results + [((depth, full), BF16)] * 2),
        in_specs=specs,
        out_specs=[hbm] * (len(results) + 2),
        scratch_shapes=[
            pltpu.VMEM((c_rows, depth), BF16),
            pltpu.VMEM((i_rows, depth), BF16),
            pltpu.VMEM((c_rows, full), BF16),
            pltpu.VMEM((i_rows, full), BF16),
            pltpu.VMEM((c_rows, full), F32),
            pltpu.VMEM((i_rows, full), F32),
            pltpu.VMEM((c_rows, 128), F32),
            pltpu.VMEM((i_rows, 128), F32),
            pltpu.VMEM((depth, full), BF16),
            pltpu.VMEM((depth, full), BF16),
            pltpu.VMEM((padded, 8), F32),
            pltpu.VMEM((img_rows, c_rows), F32),
            pltpu.VMEM((i_rows, c_rows), BF16),
            pltpu.VMEM((img_rows, full), F32),
            pltpu.VMEM((c_rows, full), F32),
            pltpu.VMEM((max(img_rows, c_rows), 128), F32),
            *(pltpu.VMEM(*kind) for kind in results),
            pltpu.SemaphoreType.DMA((n_copies,)),
        ],
        compiler_params=params(46),
        cost_estimate=cost((c_rows + i_rows) * depth * full * 2 + 3 * pair, 20),
        name="pairs",
    )(*operands)
    img_send, img_own = made[:n_send], made[n_send:n_out]
    to_core, to_next, cap_own, wc, wi = made[n_out:]

    img_sent = []
    for p in range(PARTS):
        parts = [img_send[(k - 1) * PARTS + p] for k in range(1, n_y)]
        img_sent.append([from_y(parts[k - 1], n_y - k) for k in range(1, n_y)])

    crossed = from_core(to_core)
    arrived = []
    for k in range(1, n_x):
        here = slice((k - 1) * rows, k * rows)
        sent = (to_next[here] + crossed[here].astype(F32)).astype(BF16)
        arrived.append(from_x(sent, n_x - k))
    cap_total = functools.reduce(lambda a, b: a + b.astype(F32), arrived, cap_own + crossed[others:].astype(F32))
    grad_cap = contract_last(cap_total.astype(BF16), wc).astype(BF16)

    share = depth // slots
    grad_img = []
    for p in range(PARTS):
        img_total = img_own[p]
        for arrived in img_sent[p]:
            img_total = img_total + arrived.astype(F32)
        img_part = contract_last(img_total.astype(BF16), wi)

        def columns_of(k):
            return lax.dynamic_slice_in_dim(img_part, (mine + k) % slots * share, share, axis=1)

        arrived = [from_z(columns_of(slots - k).astype(BF16), k) for k in range(1, slots)]
        grad_img.append(functools.reduce(lambda a, b: a + b.astype(F32), arrived, columns_of(0)).astype(BF16))
    return (jnp.concatenate(grad_img), grad_cap)


def solution(mesh):
    in_specs = (
        P("dp", None),
        P(("dp", "tensor"), None),
        P(None, "tensor"),
        P(None, "tensor"),
        P(),
        P(),
        P(),
    )
    out_specs = (P("dp", "tensor"), P(("dp", "tensor"), None))
    return jax.shard_map(whole, mesh=mesh, in_specs=in_specs, out_specs=out_specs, check_vma=False)
```

```python
import functools

import jax
import jax.numpy as jnp
from jax import lax
from jax.experimental import pallas as pl
from jax.experimental.pallas import tpu as pltpu
from jax.sharding import PartitionSpec as P


epsilon = 1e-06
CORES = 2
ROWS_Y = 2
CHUNK = 32
PARTS = 3
LOG2E = 1.4426950408889634
F32 = jnp.float32
BF16 = jnp.bfloat16


def contract_last(a, b):
    return lax.dot_general(a, b, (((1,), (1,)), ((), ())), preferred_element_type=F32)


def contract_first(a, b):
    return lax.dot_general(a, b, (((0,), (0,)), ((), ())), preferred_element_type=F32)


def split_rows(rows):
    units = rows // 16
    heights = [(units // PARTS + (n < units % PARTS)) * 16 for n in range(PARTS)]
    return [(sum(heights[:n]), heights[n]) for n in range(PARTS)]


def lane_sums(partial):
    ones = jnp.ones((128, 128), BF16)
    upper = partial.astype(BF16)
    lower = (partial - upper.astype(F32)).astype(BF16)
    return jnp.dot(upper, ones, preferred_element_type=F32) + jnp.dot(lower, ones, preferred_element_type=F32)


def folded(pieces):
    while len(pieces) > 1:
        pieces = [pieces[n] + pieces[n + 1] for n in range(0, len(pieces) - 1, 2)] + (
            pieces[-1:] if len(pieces) % 2 else []
        )
    return pieces[0]


def cut(ref, row, lane, height=16):
    return ref[row : row + height, lane * 128 : lane * 128 + 128]


def forward(x, w, raw, z, scales, top, rows):
    lanes = w.shape[1] // 128
    raw[top : top + rows, :] = jnp.dot(x[top : top + rows, :], w[...], preferred_element_type=F32)
    for r in range(top, top + rows, 16):
        value = [cut(raw, r, n) for n in range(lanes)]
        scales[r : r + 16, :] = folded([v * v for v in value])
    scales[top : top + rows, :] = lax.rsqrt(lane_sums(scales[top : top + rows, :]) + epsilon)
    for r in range(top, top + rows, 16):
        scale = scales[r : r + 16, :]
        for n in range(lanes):
            z[r : r + 16, n * 128 : n * 128 + 128] = (cut(raw, r, n) * scale).astype(BF16)


def back(source, raw, scales, raw_offset, offset, count, out, along):
    lanes = source.shape[1] // 128
    for r in range(offset, offset + count, 16):
        there = raw_offset + r
        along[r : r + 16, :] = folded([cut(source, r, n) * cut(raw, there, n) for n in range(lanes)])
    along[offset : offset + count, :] = lane_sums(along[offset : offset + count, :])
    for r in range(offset, offset + count, 16):
        there = raw_offset + r
        scale = scales[there : there + 16, :]
        pull = along[r : r + 16, :] * (scale * scale * scale)
        for n in range(lanes):
            value = scale * cut(source, r, n) - pull * cut(raw, there, n)
            out[r - offset : r - offset + 16, n * 128 : n * 128 + 128] = value.astype(out.dtype)


class Copies:
    def __init__(self, sem):
        self.sem, self.used = sem, 0

    def start(self, src, dst):
        copy = pltpu.make_async_copy(src, dst, self.sem.at[self.used])
        self.used += 1
        copy.start()
        return copy


def wait_all(copies):
    for copy in copies:
        copy.wait()


def place_weight(moves, own, pieces, groups, full, n_p, width, place, base):
    step = full.shape[0] // n_p
    copies = [moves.start(own, full.at[:, pl.ds(0, width)])]
    for g, group in enumerate(groups):
        for r in range(n_p):
            offset = pl.multiple_of(place[base + r], step)
            for n, k in enumerate(group):
                source = pieces[g * n_p + r].at[pl.ds(n * step, step), :]
                copies.append(moves.start(source, full.at[pl.ds(offset, step), pl.ds(k * width, width)]))
    return copies


class Operands:
    def __init__(self, refs):
        self.refs = list(refs)

    def take(self, count):
        got, self.refs = self.refs[:count], self.refs[count:]
        return got

    def one(self):
        return self.take(1)[0]


def pair_kernel(lay, *refs):
    n_cap, n_img, n_pc, n_pi = lay["n_cap"], lay["n_img"], lay["n_pc"], lay["n_pi"]
    rows, img_rows = lay["rows"], lay["img_rows"]
    groups, width = lay["groups"], lay["width"]
    args = Operands(refs)
    place, cap_x, img_x = args.one(), args.take(n_cap), args.take(n_img)
    head_c, pieces_c = args.one(), args.take(len(groups) * n_pc)
    head_i, pieces_i = args.one(), args.take(len(groups) * n_pi)
    table, position, factors = args.take(3)
    out_img = args.take(n_img * PARTS)
    out_core, out_next, out_own, out_wc, out_wi = args.take(5)
    xc, xi, zc, zi, raw_c, raw, sc_c, scales, wc, wi, bounds, logits, coef, dz, dzc, along = args.take(16)
    img_sums = args.take(n_img * PARTS)
    to_core, to_next, own, sem = args.take(4)

    moves = Copies(sem)
    heads_c = place_weight(moves, head_c, pieces_c, groups, wc, n_pc, width, place, 0)
    features_c = [moves.start(cap_x[q], xc.at[pl.ds(q * rows, rows), :]) for q in range(n_cap)]
    heads_i = place_weight(moves, head_i, pieces_i, groups, wi, n_pi, width, place, n_pc)
    features_i = [moves.start(img_x[q], xi.at[pl.ds(q * img_rows, img_rows), :]) for q in range(n_img)]
    wait_all(heads_c)
    outs = [moves.start(wc, out_wc)]
    for q in range(n_cap):
        features_c[q].wait()
        forward(xc, wc, raw_c, zc, sc_c, q * rows, rows)
    wait_all(heads_i)
    outs.append(moves.start(wi, out_wi))
    for q in range(n_img):
        features_i[q].wait()
        forward(xi, wi, raw, zi, scales, q * img_rows, img_rows)

    sharp = factors[0]
    slope, level = -LOG2E * sharp, -LOG2E * factors[1]
    spot = position[...]
    bounds[...] = jnp.transpose(table[...])
    columns = n_cap * rows
    for j in range(n_img):
        base = j * img_rows
        logits[base : base + img_rows, :] = contract_last(zi[base : base + img_rows, :], zc[...])
    for j in range(n_img):
        base = j * img_rows
        for r in range(base, base + img_rows, 16):
            bound = bounds[r : r + 16, :]
            lo, hi, plus = bound[:, 0:1], bound[:, 1:2], bound[:, 2:3]
            for c in range(0, columns, 128):
                value = logits[r : r + 16, c : c + 128] * slope + level
                col = spot[:, c : c + 128]
                inside = (col >= lo) & (col < hi)
                power = jnp.exp2(jnp.where(inside, -value, value))
                coef[r : r + 16, c : c + 128] = (jnp.where(inside, plus, sharp) / (1.0 + power)).astype(BF16)
        if j == n_img - 1:
            dzc[...] = contract_first(coef[...], zi[...])
            others = (n_cap // 2 - 1) * rows
            back(dzc, raw_c, sc_c, 0, 0, others, to_core.at[pl.ds(0, others), :], along)
            back(dzc, raw_c, sc_c, 0, 2 * others, rows, to_core.at[pl.ds(others, rows), :], along)
            outs.append(moves.start(to_core, out_core))
            if others:
                back(dzc, raw_c, sc_c, 0, others, others, to_next, along)
                outs.append(moves.start(to_next, out_next))
            back(dzc, raw_c, sc_c, 0, 2 * others + rows, rows, own, along)
            outs.append(moves.start(own, out_own))
        dz[...] = jnp.dot(coef[pl.ds(base, img_rows), :], zc[...], preferred_element_type=F32)
        for p, (top, height) in enumerate(split_rows(img_rows)):
            n = j * PARTS + p
            back(dz, raw, scales, base, top, height, img_sums[n], along)
            outs.append(moves.start(img_sums[n], out_img[n]))
    wait_all(outs)


def whole(*args):
    img_x, cap_x, img_w, cap_w, counts, sharp, shift = args
    n_dp, slots = lax.axis_size("dp"), lax.axis_size("tensor")
    n_y = ROWS_Y
    n_x = n_dp // (n_y * CORES)
    rows = cap_x.shape[0]
    img_rows = img_x.shape[0]
    depth, width = cap_w.shape
    me = lax.axis_index("dp")
    mine = lax.axis_index("tensor")
    core = me % CORES
    pos_x = (me // CORES) % n_x
    pos_y = me // (CORES * n_x)

    def number(y, x, c):
        return (y * n_x + x) * CORES + c

    def from_y(value, k):
        pairs = [
            (number((y + k) % n_y, x, c), number(y, x, c))
            for y in range(n_y)
            for x in range(n_x)
            for c in range(CORES)
        ]
        return lax.ppermute(value, "dp", pairs)

    def from_x(value, k):
        pairs = [
            (number(y, (x + k) % n_x, c), number(y, x, c))
            for y in range(n_y)
            for x in range(n_x)
            for c in range(CORES)
        ]
        return lax.ppermute(value, "dp", pairs)

    def from_core(value):
        return lax.ppermute(value, "dp", [(s, s ^ 1) for s in range(n_dp)])

    def from_z(value, k):
        return lax.ppermute(value, "tensor", [((t + k) % slots, t) for t in range(slots)])

    cap_same = [cap_x] + [from_x(cap_x, k) for k in range(1, n_x)]
    img_all = [from_y(img_x, k) for k in range(1, n_y)] + [img_x]
    cap_other = [from_core(block) for block in cap_same]
    cap_all = cap_other[1:] + cap_same[1:] + cap_other[:1] + cap_same[:1]

    n_pc, n_pi = n_x * CORES, n_y * CORES
    step_c, step_i = depth // n_pc, depth // n_pi

    def places(n_line, pos, step):
        return [((pos + j) % n_line * CORES + c) * step for c in (core, 1 - core) for j in range(n_line)]

    place = jnp.stack(places(n_x, pos_x, step_c) + places(n_y, pos_y, step_i)).astype(jnp.int32)

    ends = jnp.cumsum(counts)
    starts = ends - counts

    weights = -sharp[0] / counts.astype(F32)
    limits = jnp.stack([starts.astype(F32), ends.astype(F32), weights] + [weights] * 5)
    n_rows = n_y * img_rows
    padded = -(-n_rows // 128) * 128
    near_y = [number((pos_y + k) % n_y, pos_x, core) for k in list(range(1, n_y)) + [0]]
    table = jnp.concatenate(
        [lax.dynamic_slice_in_dim(limits, owner * img_rows, img_rows, axis=1) for owner in near_y]
        + ([jnp.zeros((8, padded - n_rows), F32)] if padded > n_rows else []),
        axis=1,
    )
    order = [(k, c) for c in (1 - core, core) for k in range(1, n_x)] + [(0, 1 - core), (0, core)]
    heads = [(number(pos_y, (pos_x + k) % n_x, c) * slots + mine) * rows for k, c in order]
    position = jnp.concatenate([head + jnp.arange(rows, dtype=jnp.int32) for head in heads]).astype(F32)[None, :]
    low = table[0, :n_rows].reshape(-1, CHUNK)[:, 0]
    high = table[1, :n_rows].reshape(-1, CHUNK)[:, -1]
    touched = functools.reduce(jnp.logical_or, [(low < head + rows) & (high > head) for head in heads])
    place = jnp.concatenate([place, touched.astype(jnp.int32)])
    factors = jnp.concatenate([sharp, shift])

    far = slots // 2
    near = [k for n in range(1, far) for k in (n, slots - n)]
    groups = [near, [far]]
    own = jnp.concatenate(
        [
            lax.dynamic_slice_in_dim(cap_w, (pos_x * CORES + core) * step_c, step_c, axis=0),
            lax.dynamic_slice_in_dim(img_w, (pos_y * CORES + core) * step_i, step_i, axis=0),
        ]
    )
    slices = {k: from_z(own, k) for k in near}
    tables = (place, table, position, factors)
    slices[far] = from_z(own, far)
    slices[near[0]], tables = lax.optimization_barrier((slices[near[0]], tables))
    place, table, position, factors = tables

    cap_pieces, img_pieces = [], []
    for group in groups:
        cap_line = [jnp.concatenate([slices[k][:step_c] for k in group])]
        img_line = [jnp.concatenate([slices[k][step_c:] for k in group])]
        cap_line += [from_x(cap_line[0], j) for j in range(1, n_x)]
        img_line += [from_y(img_line[0], j) for j in range(1, n_y)]
        cap_pieces += cap_line + [from_core(value) for value in cap_line]
        img_pieces += img_line + [from_core(value) for value in img_line]

    n_cap, n_img = n_x * CORES, n_y
    lay = dict(n_cap=n_cap, n_img=n_img, rows=rows, img_rows=img_rows, n_pc=n_pc, n_pi=n_pi, width=width)
    lay.update(groups=groups)
    full = slots * width
    c_rows, i_rows = n_cap * rows, n_img * img_rows
    hbm = pl.BlockSpec(memory_space=pltpu.HBM)
    vmem = pl.BlockSpec(memory_space=pltpu.VMEM)
    smem = pl.BlockSpec(memory_space=pltpu.SMEM)

    def of(shape, dtype):
        return jax.ShapeDtypeStruct(shape, dtype)

    def params(mib):
        return pltpu.CompilerParams(vmem_limit_bytes=mib * 2**20)

    def cost(flops, mib):
        return pl.CostEstimate(flops=flops, bytes_accessed=mib * 2**20, transcendentals=0)

    pair = 2 * c_rows * i_rows * full
    heights = [height for _, height in split_rows(img_rows)]
    n_out = n_img * PARTS
    n_copies = 2 + (slots - 1) * (n_pc + n_pi) + n_cap + n_img + n_img * PARTS + 5
    operands = [place] + cap_all + img_all + [cap_w] + cap_pieces + [img_w] + img_pieces
    specs = [smem] + [hbm] * (len(operands) - 1) + [vmem] * 2 + [smem]
    operands += [table, position, factors]
    n_send = (n_img - 1) * PARTS
    others = (n_x - 1) * rows
    results = [((heights[n % PARTS], full), BF16 if n < n_send else F32) for n in range(n_out)]
    results += [((n_x * rows, full), BF16), ((max(others, 16), full), F32), ((rows, full), F32)]
    made = pl.pallas_call(
        functools.partial(pair_kernel, lay),
        out_shape=tuple(of(*kind) for kind in results + [((depth, full), BF16)] * 2),
        in_specs=specs,
        out_specs=[hbm] * (len(results) + 2),
        scratch_shapes=[
            pltpu.VMEM((c_rows, depth), BF16),
            pltpu.VMEM((i_rows, depth), BF16),
            pltpu.VMEM((c_rows, full), BF16),
            pltpu.VMEM((i_rows, full), BF16),
            pltpu.VMEM((c_rows, full), F32),
            pltpu.VMEM((i_rows, full), F32),
            pltpu.VMEM((c_rows, 128), F32),
            pltpu.VMEM((i_rows, 128), F32),
            pltpu.VMEM((depth, full), BF16),
            pltpu.VMEM((depth, full), BF16),
            pltpu.VMEM((padded, 8), F32),
            pltpu.VMEM((i_rows, c_rows), F32),
            pltpu.VMEM((i_rows, c_rows), BF16),
            pltpu.VMEM((img_rows, full), F32),
            pltpu.VMEM((c_rows, full), F32),
            pltpu.VMEM((max(img_rows, c_rows), 128), F32),
            *(pltpu.VMEM(*kind) for kind in results),
            pltpu.SemaphoreType.DMA((n_copies,)),
        ],
        compiler_params=params(48),
        cost_estimate=cost((c_rows + i_rows) * depth * full * 2 + 3 * pair, 20),
        name="pairs",
    )(*operands)
    img_send, img_own = made[:n_send], made[n_send:n_out]
    to_core, to_next, cap_own, wc, wi = made[n_out:]

    img_sent = []
    for p in range(PARTS):
        parts = [img_send[(k - 1) * PARTS + p] for k in range(1, n_y)]
        img_sent.append([from_y(parts[k - 1], n_y - k) for k in range(1, n_y)])

    crossed = from_core(to_core)
    arrived = []
    for k in range(1, n_x):
        here = slice((k - 1) * rows, k * rows)
        sent = (to_next[here] + crossed[here].astype(F32)).astype(BF16)
        arrived.append(from_x(sent, n_x - k))
    cap_total = functools.reduce(lambda a, b: a + b.astype(F32), arrived, cap_own + crossed[others:].astype(F32))
    grad_cap = contract_last(cap_total.astype(BF16), wc).astype(BF16)

    share = depth // slots
    grad_img = []
    for p in range(PARTS):
        img_total = img_own[p]
        for arrived in img_sent[p]:
            img_total = img_total + arrived.astype(F32)
        img_part = contract_last(img_total.astype(BF16), wi)

        def columns_of(k):
            return lax.dynamic_slice_in_dim(img_part, (mine + k) % slots * share, share, axis=1)

        arrived = [from_z(columns_of(slots - k).astype(BF16), k) for k in range(1, slots)]
        grad_img.append(functools.reduce(lambda a, b: a + b.astype(F32), arrived, columns_of(0)).astype(BF16))
    return (jnp.concatenate(grad_img), grad_cap)


def solution(mesh):
    in_specs = (
        P("dp", None),
        P(("dp", "tensor"), None),
        P(None, "tensor"),
        P(None, "tensor"),
        P(),
        P(),
        P(),
    )
    out_specs = (P("dp", "tensor"), P(("dp", "tensor"), None))
    return jax.shard_map(whole, mesh=mesh, in_specs=in_specs, out_specs=out_specs, check_vma=False)
```

```python
import functools

import jax
import jax.numpy as jnp
from jax import lax
from jax.experimental import pallas as pl
from jax.experimental.pallas import tpu as pltpu
from jax.sharding import PartitionSpec as P


epsilon = 1e-06
CORES = 2
ROWS_Y = 2
PARTS = 3
LOG2E = 1.4426950408889634
F32 = jnp.float32
BF16 = jnp.bfloat16


def contract_last(a, b):
    return lax.dot_general(a, b, (((1,), (1,)), ((), ())), preferred_element_type=F32)


def contract_first(a, b):
    return lax.dot_general(a, b, (((0,), (0,)), ((), ())), preferred_element_type=F32)


def split_rows(rows):
    units = rows // 16
    heights = [(units // PARTS + (n < units % PARTS)) * 16 for n in range(PARTS)]
    return [(sum(heights[:n]), heights[n]) for n in range(PARTS)]


def lane_sums(partial):
    ones = jnp.ones((128, 128), BF16)
    upper = partial.astype(BF16)
    lower = (partial - upper.astype(F32)).astype(BF16)
    return jnp.dot(upper, ones, preferred_element_type=F32) + jnp.dot(lower, ones, preferred_element_type=F32)


def folded(pieces):
    while len(pieces) > 1:
        pieces = [pieces[n] + pieces[n + 1] for n in range(0, len(pieces) - 1, 2)] + (
            pieces[-1:] if len(pieces) % 2 else []
        )
    return pieces[0]


def cut(ref, row, lane, height=16):
    return ref[row : row + height, lane * 128 : lane * 128 + 128]


def forward(x, w, raw, z, scales, top, rows):
    lanes = w.shape[1] // 128
    raw[top : top + rows, :] = jnp.dot(x[top : top + rows, :], w[...], preferred_element_type=F32)
    for r in range(top, top + rows, 16):
        value = [cut(raw, r, n) for n in range(lanes)]
        scales[r : r + 16, :] = folded([v * v for v in value])
    scales[top : top + rows, :] = lax.rsqrt(lane_sums(scales[top : top + rows, :]) + epsilon)
    for r in range(top, top + rows, 16):
        scale = scales[r : r + 16, :]
        for n in range(lanes):
            z[r : r + 16, n * 128 : n * 128 + 128] = (cut(raw, r, n) * scale).astype(BF16)


def back(source, raw, scales, raw_offset, offset, count, out, along):
    lanes = source.shape[1] // 128
    for r in range(offset, offset + count, 16):
        there = raw_offset + r
        along[r : r + 16, :] = folded([cut(source, r, n) * cut(raw, there, n) for n in range(lanes)])
    along[offset : offset + count, :] = lane_sums(along[offset : offset + count, :])
    for r in range(offset, offset + count, 16):
        there = raw_offset + r
        scale = scales[there : there + 16, :]
        pull = along[r : r + 16, :] * (scale * scale * scale)
        for n in range(lanes):
            value = scale * cut(source, r, n) - pull * cut(raw, there, n)
            out[r - offset : r - offset + 16, n * 128 : n * 128 + 128] = value.astype(out.dtype)


class Copies:
    def __init__(self, sem):
        self.sem, self.used = sem, 0

    def start(self, src, dst):
        copy = pltpu.make_async_copy(src, dst, self.sem.at[self.used])
        self.used += 1
        copy.start()
        return copy


def wait_all(copies):
    for copy in copies:
        copy.wait()


def place_weight(moves, own, pieces, groups, full, n_p, width, place, base):
    step = full.shape[0] // n_p
    copies = [moves.start(own, full.at[:, pl.ds(0, width)])]
    for g, group in enumerate(groups):
        for r in range(n_p):
            offset = pl.multiple_of(place[base + r], step)
            for n, k in enumerate(group):
                source = pieces[g * n_p + r].at[pl.ds(n * step, step), :]
                copies.append(moves.start(source, full.at[pl.ds(offset, step), pl.ds(k * width, width)]))
    return copies


class Operands:
    def __init__(self, refs):
        self.refs = list(refs)

    def take(self, count):
        got, self.refs = self.refs[:count], self.refs[count:]
        return got

    def one(self):
        return self.take(1)[0]


def pair_kernel(lay, *refs):
    n_cap, n_img, n_pc, n_pi = lay["n_cap"], lay["n_img"], lay["n_pc"], lay["n_pi"]
    rows, img_rows = lay["rows"], lay["img_rows"]
    groups, width = lay["groups"], lay["width"]
    args = Operands(refs)
    place, cap_x, img_x = args.one(), args.take(n_cap), args.take(n_img)
    head_c, pieces_c = args.one(), args.take(len(groups) * n_pc)
    head_i, pieces_i = args.one(), args.take(len(groups) * n_pi)
    table, position, factors = args.take(3)
    out_img = args.take(n_img * PARTS)
    out_core, out_next, out_own, out_wc, out_wi = args.take(5)
    xc, xi, zc, zi, raw_c, raw, sc_c, scales, wc, wi, bounds, logits, coef, dz, dzc, along = args.take(16)
    img_sums = args.take(n_img * PARTS)
    to_core, to_next, own, sem = args.take(4)

    moves = Copies(sem)
    heads_c = place_weight(moves, head_c, pieces_c, groups, wc, n_pc, width, place, 0)
    features_c = [moves.start(cap_x[q], xc.at[pl.ds(q * rows, rows), :]) for q in range(n_cap)]
    heads_i = place_weight(moves, head_i, pieces_i, groups, wi, n_pi, width, place, n_pc)
    features_i = [moves.start(img_x[q], xi.at[pl.ds(q * img_rows, img_rows), :]) for q in range(n_img)]
    wait_all(heads_c)
    outs = [moves.start(wc, out_wc)]
    for q in range(n_cap):
        features_c[q].wait()
        forward(xc, wc, raw_c, zc, sc_c, q * rows, rows)
    wait_all(heads_i)
    outs.append(moves.start(wi, out_wi))
    for q in range(n_img):
        features_i[q].wait()
        forward(xi, wi, raw, zi, scales, q * img_rows, img_rows)

    sharp = factors[0]
    slope, level = -LOG2E * sharp, -LOG2E * factors[1]
    spot = position[...]
    bounds[...] = jnp.transpose(table[...])
    columns = n_cap * rows
    for j in range(n_img):
        base = j * img_rows
        logits[base : base + img_rows, :] = contract_last(zi[base : base + img_rows, :], zc[...])
    for j in range(n_img):
        base = j * img_rows
        for r in range(base, base + img_rows, 16):
            bound = bounds[r : r + 16, :]
            lo, hi, plus = bound[:, 0:1], bound[:, 1:2], bound[:, 2:3]
            for c in range(0, columns, 128):
                value = logits[r : r + 16, c : c + 128] * slope + level
                col = spot[:, c : c + 128]
                inside = (col >= lo) & (col < hi)
                power = jnp.exp2(jnp.where(inside, -value, value))
                coef[r : r + 16, c : c + 128] = (jnp.where(inside, plus, sharp) / (1.0 + power)).astype(BF16)
        if j == n_img - 1:
            dzc[...] = contract_first(coef[...], zi[...])
            others = (n_cap // 2 - 1) * rows
            back(dzc, raw_c, sc_c, 0, 0, others, to_core.at[pl.ds(0, others), :], along)
            back(dzc, raw_c, sc_c, 0, 2 * others, rows, to_core.at[pl.ds(others, rows), :], along)
            outs.append(moves.start(to_core, out_core))
            if others:
                back(dzc, raw_c, sc_c, 0, others, others, to_next, along)
                outs.append(moves.start(to_next, out_next))
            back(dzc, raw_c, sc_c, 0, 2 * others + rows, rows, own, along)
            outs.append(moves.start(own, out_own))
        dz[...] = jnp.dot(coef[pl.ds(base, img_rows), :], zc[...], preferred_element_type=F32)
        for p, (top, height) in enumerate(split_rows(img_rows)):
            n = j * PARTS + p
            back(dz, raw, scales, base, top, height, img_sums[n], along)
            outs.append(moves.start(img_sums[n], out_img[n]))
    wait_all(outs)


def whole(*args):
    img_x, cap_x, img_w, cap_w, counts, sharp, shift = args
    n_dp, slots = lax.axis_size("dp"), lax.axis_size("tensor")
    n_y = ROWS_Y
    n_x = n_dp // (n_y * CORES)
    rows = cap_x.shape[0]
    img_rows = img_x.shape[0]
    depth, width = cap_w.shape
    me = lax.axis_index("dp")
    mine = lax.axis_index("tensor")
    core = me % CORES
    pos_x = (me // CORES) % n_x
    pos_y = me // (CORES * n_x)

    def number(y, x, c):
        return (y * n_x + x) * CORES + c

    def from_y(value, k):
        pairs = [
            (number((y + k) % n_y, x, c), number(y, x, c))
            for y in range(n_y)
            for x in range(n_x)
            for c in range(CORES)
        ]
        return lax.ppermute(value, "dp", pairs)

    def from_x(value, k):
        pairs = [
            (number(y, (x + k) % n_x, c), number(y, x, c))
            for y in range(n_y)
            for x in range(n_x)
            for c in range(CORES)
        ]
        return lax.ppermute(value, "dp", pairs)

    def from_core(value):
        return lax.ppermute(value, "dp", [(s, s ^ 1) for s in range(n_dp)])

    def from_z(value, k):
        return lax.ppermute(value, "tensor", [((t + k) % slots, t) for t in range(slots)])

    cap_same = [cap_x] + [from_x(cap_x, k) for k in range(1, n_x)]
    img_all = [from_y(img_x, k) for k in range(1, n_y)] + [img_x]
    cap_other = [from_core(block) for block in cap_same]
    cap_all = cap_other[1:] + cap_same[1:] + cap_other[:1] + cap_same[:1]

    n_pc, n_pi = n_x * CORES, n_y * CORES
    step_c, step_i = depth // n_pc, depth // n_pi

    def places(n_line, pos, step):
        return [((pos + j) % n_line * CORES + c) * step for c in (core, 1 - core) for j in range(n_line)]

    place = jnp.stack(places(n_x, pos_x, step_c) + places(n_y, pos_y, step_i)).astype(jnp.int32)

    ends = jnp.cumsum(counts)
    starts = ends - counts

    weights = -sharp[0] / counts.astype(F32)
    limits = jnp.stack([starts.astype(F32), ends.astype(F32), weights] + [weights] * 5)
    n_rows = n_y * img_rows
    padded = -(-n_rows // 128) * 128
    near_y = [number((pos_y + k) % n_y, pos_x, core) for k in list(range(1, n_y)) + [0]]
    table = jnp.concatenate(
        [lax.dynamic_slice_in_dim(limits, owner * img_rows, img_rows, axis=1) for owner in near_y]
        + ([jnp.zeros((8, padded - n_rows), F32)] if padded > n_rows else []),
        axis=1,
    )
    order = [(k, c) for c in (1 - core, core) for k in range(1, n_x)] + [(0, 1 - core), (0, core)]
    heads = [(number(pos_y, (pos_x + k) % n_x, c) * slots + mine) * rows for k, c in order]
    position = jnp.concatenate([head + jnp.arange(rows, dtype=jnp.int32) for head in heads]).astype(F32)[None, :]
    factors = jnp.concatenate([sharp, shift])

    far = slots // 2
    near = [k for n in range(1, far) for k in (n, slots - n)]
    groups = [near, [far]]
    own = jnp.concatenate(
        [
            lax.dynamic_slice_in_dim(cap_w, (pos_x * CORES + core) * step_c, step_c, axis=0),
            lax.dynamic_slice_in_dim(img_w, (pos_y * CORES + core) * step_i, step_i, axis=0),
        ]
    )
    slices = {k: from_z(own, k) for k in near}
    tables = (place, table, position, factors)
    slices[far] = from_z(own, far)
    slices[near[0]], tables = lax.optimization_barrier((slices[near[0]], tables))
    place, table, position, factors = tables

    cap_pieces, img_pieces = [], []
    for group in groups:
        cap_line = [jnp.concatenate([slices[k][:step_c] for k in group])]
        img_line = [jnp.concatenate([slices[k][step_c:] for k in group])]
        cap_line += [from_x(cap_line[0], j) for j in range(1, n_x)]
        img_line += [from_y(img_line[0], j) for j in range(1, n_y)]
        cap_pieces += cap_line + [from_core(value) for value in cap_line]
        img_pieces += img_line + [from_core(value) for value in img_line]

    n_cap, n_img = n_x * CORES, n_y
    lay = dict(n_cap=n_cap, n_img=n_img, rows=rows, img_rows=img_rows, n_pc=n_pc, n_pi=n_pi, width=width)
    lay.update(groups=groups)
    full = slots * width
    c_rows, i_rows = n_cap * rows, n_img * img_rows
    hbm = pl.BlockSpec(memory_space=pltpu.HBM)
    vmem = pl.BlockSpec(memory_space=pltpu.VMEM)
    smem = pl.BlockSpec(memory_space=pltpu.SMEM)

    def of(shape, dtype):
        return jax.ShapeDtypeStruct(shape, dtype)

    def params(mib):
        return pltpu.CompilerParams(vmem_limit_bytes=mib * 2**20)

    def cost(flops, mib):
        return pl.CostEstimate(flops=flops, bytes_accessed=mib * 2**20, transcendentals=0)

    pair = 2 * c_rows * i_rows * full
    heights = [height for _, height in split_rows(img_rows)]
    n_out = n_img * PARTS
    n_copies = 2 + (slots - 1) * (n_pc + n_pi) + n_cap + n_img + n_img * PARTS + 5
    operands = [place] + cap_all + img_all + [cap_w] + cap_pieces + [img_w] + img_pieces
    specs = [smem] + [hbm] * (len(operands) - 1) + [vmem] * 2 + [smem]
    operands += [table, position, factors]
    n_send = (n_img - 1) * PARTS
    others = (n_x - 1) * rows
    results = [((heights[n % PARTS], full), BF16 if n < n_send else F32) for n in range(n_out)]
    results += [((n_x * rows, full), BF16), ((max(others, 16), full), F32), ((rows, full), F32)]
    made = pl.pallas_call(
        functools.partial(pair_kernel, lay),
        out_shape=tuple(of(*kind) for kind in results + [((depth, full), BF16)] * 2),
        in_specs=specs,
        out_specs=[hbm] * (len(results) + 2),
        scratch_shapes=[
            pltpu.VMEM((c_rows, depth), BF16),
            pltpu.VMEM((i_rows, depth), BF16),
            pltpu.VMEM((c_rows, full), BF16),
            pltpu.VMEM((i_rows, full), BF16),
            pltpu.VMEM((c_rows, full), F32),
            pltpu.VMEM((i_rows, full), F32),
            pltpu.VMEM((c_rows, 128), F32),
            pltpu.VMEM((i_rows, 128), F32),
            pltpu.VMEM((depth, full), BF16),
            pltpu.VMEM((depth, full), BF16),
            pltpu.VMEM((padded, 8), F32),
            pltpu.VMEM((i_rows, c_rows), F32),
            pltpu.VMEM((i_rows, c_rows), BF16),
            pltpu.VMEM((img_rows, full), F32),
            pltpu.VMEM((c_rows, full), F32),
            pltpu.VMEM((max(img_rows, c_rows), 128), F32),
            *(pltpu.VMEM(*kind) for kind in results),
            pltpu.SemaphoreType.DMA((n_copies,)),
        ],
        compiler_params=params(47),
        cost_estimate=cost((c_rows + i_rows) * depth * full * 2 + 3 * pair, 20),
        name="pairs",
    )(*operands)
    img_send, img_own = made[:n_send], made[n_send:n_out]
    to_core, to_next, cap_own, wc, wi = made[n_out:]

    img_sent = []
    for p in range(PARTS):
        parts = [img_send[(k - 1) * PARTS + p] for k in range(1, n_y)]
        img_sent.append([from_y(parts[k - 1], n_y - k) for k in range(1, n_y)])

    crossed = from_core(to_core)
    arrived = []
    for k in range(1, n_x):
        here = slice((k - 1) * rows, k * rows)
        sent = (to_next[here] + crossed[here].astype(F32)).astype(BF16)
        arrived.append(from_x(sent, n_x - k))
    cap_total = functools.reduce(lambda a, b: a + b.astype(F32), arrived, cap_own + crossed[others:].astype(F32))
    grad_cap = contract_last(cap_total.astype(BF16), wc).astype(BF16)

    share = depth // slots
    grad_img = []
    for p in range(PARTS):
        img_total = img_own[p]
        for arrived in img_sent[p]:
            img_total = img_total + arrived.astype(F32)
        img_part = contract_last(img_total.astype(BF16), wi)

        def columns_of(k):
            return lax.dynamic_slice_in_dim(img_part, (mine + k) % slots * share, share, axis=1)

        arrived = [from_z(columns_of(slots - k).astype(BF16), k) for k in range(1, slots)]
        grad_img.append(functools.reduce(lambda a, b: a + b.astype(F32), arrived, columns_of(0)).astype(BF16))
    return (jnp.concatenate(grad_img), grad_cap)


def solution(mesh):
    in_specs = (
        P("dp", None),
        P(("dp", "tensor"), None),
        P(None, "tensor"),
        P(None, "tensor"),
        P(),
        P(),
        P(),
    )
    out_specs = (P("dp", "tensor"), P(("dp", "tensor"), None))
    return jax.shard_map(whole, mesh=mesh, in_specs=in_specs, out_specs=out_specs, check_vma=False)
```
